512 devices in a mesh: gz: 16 (over y, x), pa: 32 (over z, core).
Axes of the slice: x: 4, y: 4, z: 16, core: 2. Of those that a mesh axis runs over, the one named last changes fastest.
Arguments:
- particles: float32 [6, 1048576], P(None, ('gz', 'pa')), may hold values from -6 to 6
- slice_index: int32 [1048576], P(('gz', 'pa')), may hold values from 0 to 127
- moving: int32 [16, 32, 2], P('gz', 'pa'), may hold values from 0 to 384, as said below
- decay_rate: float32 [8], replicated, may hold values from 0.3 to 600
- wake_freq: float32 [8], replicated, may hold values from -3.140625 to 3.140625
- wake_amp: float32 [4, 8], replicated, may hold values from -3 to 3
Outputs:
- wake_kick: float32 [3, 2048], P(None, 'gz')
- particles_out: float32 [6, 1441792], P(None, ('gz', 'pa'))
The draws below stay inside these ranges and needn't reach their ends.
Inputs may be any that keep to these rules, and one draw needn't show every extreme that they name: `moving`: each entry is at most 384, and some entry equals 384.
All inputs are finite; a program needn't handle non-finite values.
Results may differ from the reference program's by a relative error of at most 0.0003.
Values sent between devices are 32-bit elements; how exact they have to be, the bound alone decides.
No kernel may reach another device: no remote copies, remote signals or barrier semaphores. Data moves between devices by JAX's collectives and lax.ppermute only.
A program may use at most 64 MiB of HBM per device.

```python
import math
import jax
import jax.numpy as jnp
import numpy as np
from jax import lax

S_DEV = 128
P_DEV = 2048
MODES = 8
CAP = 384
NSLICE = 2048
NPART = 1048576
N_GZ = 16
N_PA = 32


def draw_moving(key, part):
    first_key, second_key = jax.random.split(key)
    counts = jax.random.randint(first_key, (N_GZ * N_PA * 2,), 0, CAP + 1)
    chosen = jax.random.randint(second_key, (), 0, N_GZ * N_PA * 2)
    counts = counts.at[chosen].set(CAP)
    return counts.reshape(N_GZ, N_PA, 2).astype(jnp.int32)


def place_ends(entries, own_key, smallest, high):
    longest = entries.shape.index(max(entries.shape))
    spots = []
    for shift in (0, 1):
        where = [jax.random.randint(jax.random.fold_in(own_key, axis), (), 0, length) for axis, length in enumerate(entries.shape)]
        where[longest] = (where[longest] + shift) % entries.shape[longest]
        spots.append(tuple(where))
    return entries.at[spots[0]].set(smallest).at[spots[1]].set(high)


def steps_of(stream_key, extent, cuts, least, largest):
    def one(position, shards_of):
        steps = jax.random.uniform(jax.random.fold_in(jax.random.fold_in(stream_key, 6), position), (shards_of,), jnp.float32, least / len(cuts), largest / len(cuts))
        return jnp.repeat(jnp.exp(steps), extent[position] // shards_of).reshape((-1,) + (1,) * (len(extent) - position - 1))

    gain = one(*cuts[0])
    for cut in cuts[1:]:
        gain = gain * one(*cut)
    return gain


def rank_table(count, lean):
    loads = [(1 << 20) // math.isqrt(grade ** lean) + 1 for grade in range(1, count + 1)]
    width = 1 + sum(loads) // (1 << 30)
    return np.cumsum(np.array([max(1, weight // width) for weight in loads]))


def ranked_ids(stream_key, extent, number_of, lean):
    table = rank_table(number_of, lean)
    ticket = jax.random.randint(jax.random.fold_in(stream_key, 1), extent, 0, int(table[number_of - 1]))
    standing = jnp.searchsorted(jnp.asarray(table, jnp.int32), ticket, side="right")
    return jax.random.permutation(jax.random.fold_in(stream_key, 2), number_of)[standing].astype(jnp.int32)


def noise(rng, dims, width, limit, cuts=(), held_as=jnp.bfloat16):
    factor_of = steps_of(rng, dims, cuts, -0.22, 0.18) if cuts else 1.0
    values = jax.random.normal(rng, dims, jnp.float32) * width * factor_of
    return jnp.minimum(jnp.maximum(values, -limit), limit).astype(held_as)


def setup_inputs(seed: int = 0) -> dict:
    seeds = jax.random.split(jax.random.key(seed), 7)
    particles = noise(seeds[0], (6, NPART), 1.0, 6.0, ((1, 512),), jnp.float32)
    slice_index = place_ends(ranked_ids(seeds[1], (NPART,), S_DEV, 1), jax.random.fold_in(seeds[1], 3), 0, S_DEV - 1).astype(jnp.int32)
    moving = draw_moving(jax.random.fold_in(seeds[6], 71), 0)
    decay_rate = jnp.clip(jnp.exp(jax.random.uniform(seeds[3], (MODES,), jnp.float32, math.log(0.3), math.log(600.0))), 0.3, 600.0)
    wake_freq = jnp.clip(jax.random.uniform(seeds[4], (MODES,), jnp.float32, -3.140625, 3.140625), -3.140625, 3.140625)
    wake_amp = noise(seeds[5], (4, MODES), 0.5, 3.0, (), jnp.float32)
    return dict(particles=particles, slice_index=slice_index, moving=moving, decay_rate=decay_rate, wake_freq=wake_freq, wake_amp=wake_amp)


two_pi = 6.283185307179586
adjust_horiz = 0.269
adjust_vert = 0.355
chroma_horiz = 0.05
chroma_vert = 0.04
curve_horiz = 0.02
curve_vert = -0.015
detune_self = 0.03
detune_cross = -0.02
voltage = 0.05
synch_phase = 0.3
slippage = 0.1

def complex_mul(first, second):
    return jnp.stack([first[0] * second[0] - first[1] * second[1], first[0] * second[1] + first[1] * second[0]])

def powers(damping, wake_freq, distance):
    envelope = jnp.exp(-damping[:, None] * distance[None, :])
    angles = wake_freq[:, None] * distance[None, :]
    return (envelope * jnp.cos(angles), envelope * jnp.sin(angles))

def toeplitz(wave):
    slab_width = wave.shape[0]
    row_index = lax.broadcasted_iota(jnp.int32, (slab_width, slab_width), 0)
    col_index = lax.broadcasted_iota(jnp.int32, (slab_width, slab_width), 1)
    offset = col_index - row_index
    picked = jnp.take(wave, jnp.clip(offset, 0, slab_width - 1))
    return jnp.where(offset > 0, picked, jnp.float32(0.0))

def slab_tables(decay_rate, wake_freq, wake_amp, slab_width, slice_total):
    damping = decay_rate / slice_total
    norm_trans = jnp.sqrt(2.0 * damping)
    norm_long = jnp.sqrt(damping * damping + wake_freq * wake_freq)
    coef_real = jnp.stack([wake_amp[0] * norm_trans, wake_amp[0] * norm_trans, wake_amp[2] * norm_long], axis=1)
    coef_imag = jnp.stack([wake_amp[1] * norm_trans, wake_amp[1] * norm_trans, wake_amp[3] * norm_long], axis=1)
    distance = jnp.arange(slab_width, dtype=jnp.float32)
    near_re, near_im = powers(damping, wake_freq, distance)
    far_re, far_im = powers(damping, wake_freq, slab_width - distance)
    whole_re, whole_im = powers(damping, wake_freq, jnp.full((1,), slab_width, jnp.float32))
    factor = jnp.stack([jnp.broadcast_to(whole_re, coef_real.shape), jnp.broadcast_to(whole_im, coef_real.shape)])
    wave_trans = lax.optimization_barrier(jnp.sum(norm_trans[:, None] * (wake_amp[0][:, None] * near_re - wake_amp[1][:, None] * near_im), axis=0))
    wave_long = lax.optimization_barrier(jnp.sum(norm_long[:, None] * (wake_amp[2][:, None] * near_re - wake_amp[3][:, None] * near_im), axis=0))
    return (toeplitz(wave_trans), toeplitz(wave_long), near_re, near_im, far_re, far_im, factor, coef_real, coef_imag)

def slab_summary(moments, tables):
    highest = lax.Precision.HIGHEST
    return jnp.stack([jnp.dot(tables[4], moments.T, precision=highest), jnp.dot(tables[5], moments.T, precision=highest)])

def slab_kick(moments, carried, tables):
    highest = lax.Precision.HIGHEST
    trans_kick = jnp.dot(moments[0:2], tables[0], precision=highest)
    long_kick = jnp.dot(moments[2:3], tables[1], precision=highest)
    coef_re = tables[7] * carried[0] - tables[8] * carried[1]
    coef_im = tables[7] * carried[1] + tables[8] * carried[0]
    incoming = jnp.dot(coef_re.T, tables[2], precision=highest) - jnp.dot(coef_im.T, tables[3], precision=highest)
    return jnp.concatenate([trans_kick, long_kick], axis=0) + incoming

def moment_values(particles, mean_fill):
    root_fill = math.sqrt(mean_fill)
    return jnp.stack([particles[0] / root_fill, particles[2] / root_fill, jnp.full_like(particles[0], 1.0 / mean_fill)])

def deposit(values, index, segments):
    return jax.vmap(lambda column: jax.ops.segment_sum(column, index, num_segments=segments))(values)

def one_turn(coords, kicks):
    hor_pos = coords[0]
    hor_mom = coords[1] + kicks[0]
    ver_pos = coords[2]
    ver_mom = coords[3] + kicks[1]
    lag_pos = coords[4]
    energy_dev = coords[5] + kicks[2]
    action_x = 0.5 * (hor_pos * hor_pos + hor_mom * hor_mom)
    action_y = 0.5 * (ver_pos * ver_pos + ver_mom * ver_mom)
    phase_x = two_pi * (adjust_horiz + chroma_horiz * energy_dev + curve_horiz * energy_dev * energy_dev + detune_self * action_x + detune_cross * action_y)
    phase_y = two_pi * (adjust_vert + chroma_vert * energy_dev + curve_vert * energy_dev * energy_dev + detune_self * action_y + detune_cross * action_x)
    cosine_x = jnp.cos(phase_x)
    sine_x = jnp.sin(phase_x)
    cosine_y = jnp.cos(phase_y)
    sine_y = jnp.sin(phase_y)
    new_energy = energy_dev - voltage * (jnp.sin(synch_phase + lag_pos) - math.sin(synch_phase))
    new_lag = lag_pos - slippage * new_energy
    return jnp.stack([cosine_x * hor_pos + sine_x * hor_mom, cosine_x * hor_mom - sine_x * hor_pos, cosine_y * ver_pos + sine_y * ver_mom, cosine_y * ver_mom - sine_y * ver_pos, new_lag, new_energy])

def reference(particles, slice_index, moving, decay_rate, wake_freq, wake_amp):
    per_slab = N_PA * P_DEV
    mean_fill = P_DEV * N_PA / S_DEV
    tables = slab_tables(decay_rate, wake_freq, wake_amp, S_DEV, NSLICE)
    global_slice = (slice_index.reshape(N_GZ, per_slab) + (jnp.arange(N_GZ, dtype=jnp.int32) * S_DEV)[:, None]).reshape(-1)
    moments = deposit(moment_values(particles, mean_fill), global_slice, NSLICE)
    slabs_moments = moments.reshape(3, N_GZ, S_DEV).transpose(1, 0, 2)
    summaries = jax.vmap(lambda block: slab_summary(block, tables))(slabs_moments)

    def advance(carried, own_summary):
        return (complex_mul(tables[6], carried) + own_summary, carried)
    _, incoming_all = lax.scan(advance, jnp.zeros_like(summaries[0]), summaries)
    kicks = jax.vmap(lambda block, carried: slab_kick(block, carried, tables))(slabs_moments, incoming_all)
    wake_kick = kicks.transpose(1, 0, 2).reshape(3, NSLICE)
    per_particle = jnp.take(wake_kick, global_slice, axis=1)
    moved_all = one_turn(particles, per_particle)
    blocks = moved_all.reshape(6, N_GZ, N_PA, P_DEV)
    head_count = moving[:, :, 0][None, :, :, None]
    tail_count = moving[:, :, 1][None, :, :, None]
    slot_index = jnp.arange(P_DEV, dtype=jnp.int32)
    leaving_head = slot_index < head_count
    leaving_tail = slot_index >= P_DEV - tail_count
    kept_part = jnp.where(leaving_head | leaving_tail, jnp.float32(0.0), blocks)
    head_send = jnp.where(leaving_head, blocks, jnp.float32(0.0))[..., :CAP]
    tail_send = jnp.where(leaving_tail, blocks, jnp.float32(0.0))[..., P_DEV - CAP:]
    from_behind = jnp.concatenate([head_send[:, 1:], jnp.zeros_like(head_send[:, :1])], axis=1)
    from_ahead = jnp.concatenate([jnp.zeros_like(tail_send[:, :1]), tail_send[:, :-1]], axis=1)
    particles_out = jnp.concatenate([from_behind, kept_part, from_ahead], axis=3).reshape(6, -1)
    return (wake_kick, particles_out)
```

```python
import functools
import math

import jax
import jax.numpy as jnp
from jax import lax
from jax.experimental import pallas as pl
from jax.experimental.pallas import tpu as pltpu
from jax.sharding import PartitionSpec as P

LANES = 128
MODES = 8
ROWS = 24
HIGH = lax.Precision.HIGHEST
F32 = jnp.float32

COS_TERMS = (1.0, -19.73920440673828, 64.93911743164062, -85.45014190673828, 60.167633056640625,
             -25.967601776123047, 6.528658866882324)
SIN_TERMS = (6.2831854820251465, -41.34170150756836, 81.60513305664062, -76.70301818847656,
             42.02592849731445, -14.899847984313965, 3.238137722015381)
INV_TWO_PI = 0.15915494309189535
TURN_PARTS = (6.28125, 1.93500518798828125e-3, 3.0199159819567529e-7)


def horner(terms, t):
    total = jnp.full_like(t, terms[-1])
    for term in terms[-2::-1]:
        total = total * t + F32(term)
    return total


def turn_reduce(turns):
    return turns - jnp.floor(turns + F32(0.5))


def sine(turns):
    return turns * horner(SIN_TERMS, turns * turns)


def cosine(turns):
    return horner(COS_TERMS, turns * turns)


def radians_to_turns(angle):
    whole = jnp.floor(angle * F32(INV_TWO_PI) + F32(0.5))
    rest = angle
    for part in TURN_PARTS:
        rest = rest - whole * F32(part)
    return rest * F32(INV_TWO_PI)


def powers(damping, freq, distance):
    envelope = jnp.exp(-damping * distance)
    turns = radians_to_turns(freq * distance)
    return envelope * cosine(turns), envelope * sine(turns)


def complex_mul(a, b):
    return a[0] * b[0] - a[1] * b[1], a[0] * b[1] + a[1] * b[0]


def spread(read, shape, axis):
    where = lax.broadcasted_iota(jnp.int32, shape, axis)
    total = jnp.zeros(shape, F32)
    for mode in range(MODES):
        total = jnp.where(where == mode, read(mode), total)
    return total


def tables_kernel(slabs, width, slab_ref, decay_ref, freq_ref, amp_ref, near_ref, far_ref, trans_ref, long_ref, hop_ref, coef_ref):
    shape = (MODES, LANES)
    scale = F32(1.0 / (slabs * width))
    damping = spread(lambda m: decay_ref[m], shape, 0) * scale
    freq = spread(lambda m: freq_ref[m], shape, 0)
    amps = [spread(functools.partial(lambda row, m: amp_ref[row, m], row), shape, 0) for row in range(4)]
    distance = lax.broadcasted_iota(jnp.int32, shape, 1).astype(F32)
    near = powers(damping, freq, distance)
    far = powers(damping, freq, F32(width) - distance)
    near_ref[0:8, :] = near[0]
    near_ref[8:16, :] = near[1]
    far_ref[0:8, :] = far[0]
    far_ref[8:16, :] = far[1]
    norm_trans = jnp.sqrt(2.0 * damping)
    norm_long = jnp.sqrt(damping * damping + freq * freq)
    wave_trans = jnp.sum(norm_trans * (amps[0] * near[0] - amps[1] * near[1]), axis=0, keepdims=True)
    wave_long = jnp.sum(norm_long * (amps[2] * near[0] - amps[3] * near[1]), axis=0, keepdims=True)
    square = (LANES, LANES)
    later = lax.broadcasted_iota(jnp.int32, square, 1) > lax.broadcasted_iota(jnp.int32, square, 0)
    for wave, ref in ((wave_trans, trans_ref), (wave_long, long_ref)):
        shifted = pltpu.roll(jnp.broadcast_to(wave, square), 0, 1, stride=1, stride_axis=0)
        ref[...] = jnp.where(later, shifted, F32(0.0))

    small = (slabs, MODES)
    damping = spread(lambda m: decay_ref[m], small, 1) * scale
    freq = spread(lambda m: freq_ref[m], small, 1)
    amps = [spread(functools.partial(lambda row, m: amp_ref[row, m], row), small, 1) for row in range(4)]
    norm_trans = jnp.sqrt(2.0 * damping)
    norm_long = jnp.sqrt(damping * damping + freq * freq)
    coef_ref[0] = amps[0] * norm_trans
    coef_ref[1] = amps[1] * norm_trans
    coef_ref[2] = amps[2] * norm_long
    coef_ref[3] = amps[3] * norm_long
    step = powers(damping, freq, jnp.full(small, width, F32))
    ladder = [step]
    while 2 ** len(ladder) < slabs:
        ladder.append(complex_mul(ladder[-1], ladder[-1]))
    source = lax.broadcasted_iota(jnp.int32, small, 0)
    for index in range(3):
        hops = slab_ref[0] + (index - 2) - source
        weight = (jnp.ones(small, F32), jnp.zeros(small, F32))
        for bit, factor in enumerate(ladder):
            longer = complex_mul(weight, factor)
            taken = (hops & (1 << bit)) != 0
            weight = tuple(jnp.where(taken, b, a) for a, b in zip(weight, longer))
        ahead = hops >= 0
        hop_ref[2 * index] = jnp.where(ahead, weight[0], F32(0.0))
        hop_ref[2 * index + 1] = jnp.where(ahead, weight[1], F32(0.0))


def deposit_kernel(local, capacity, fill, part_ref, index_ref, moving_ref, moment_ref, dense_ref, head_ref, tail_ref):
    tiles = local // LANES
    shape = (8, local)
    row = lax.broadcasted_iota(jnp.int32, shape, 0)
    base = jnp.where(row < 3, part_ref[0:1, :], jnp.where(row < 6, part_ref[2:3, :], F32(1.0)))
    bf = jnp.bfloat16
    high = base.astype(bf).astype(F32)
    rest = base - high
    mid = rest.astype(bf).astype(F32)
    low = rest - mid
    third = row % 3
    values = jnp.where(third == 0, high, jnp.where(third == 1, mid, low)).astype(bf)
    slot = lax.broadcasted_iota(jnp.int32, (LANES, LANES), 0)
    total = jnp.zeros((8, LANES), F32)
    group = 2
    for first in range(0, tiles, group):
        hot = jnp.concatenate(
            [(slot == index_ref[t:t + 1, :]).astype(F32).astype(bf) for t in range(first, first + group)], axis=1
        )
        total = total + lax.dot_general(
            values[:, first * LANES:(first + group) * LANES], hot, (((1,), (1,)), ((), ())), preferred_element_type=F32
        )
    root = F32(1.0 / math.sqrt(fill))
    moment_ref[0:1, :] = (total[0:1] + total[1:2] + total[2:3]) * root
    moment_ref[1:2, :] = (total[3:4] + total[4:5] + total[5:6]) * root
    moment_ref[2:3, :] = total[6:7] * F32(1.0 / fill)
    moment_ref[3:4, :] = jnp.zeros((1, LANES), F32)

    for tile in range(tiles):
        dense_ref[pl.ds(tile, 6, stride=tiles), :] = part_ref[:, tile * LANES:(tile + 1) * LANES]
    edge = capacity // LANES
    place = lax.broadcasted_iota(jnp.int32, (edge, LANES), 0) * LANES + lax.broadcasted_iota(jnp.int32, (edge, LANES), 1)
    for ref, start, leaving in (
        (head_ref, 0, place < moving_ref[0, 0, 0]),
        (tail_ref, tiles - edge, place >= capacity - moving_ref[0, 0, 1]),
    ):
        ref[0:edge, :] = jnp.zeros((edge, LANES), F32)
        for q in range(6):
            ref[edge * (q + 1):edge * (q + 2), :] = dense_ref[q * tiles + start:q * tiles + start + edge, :]
        ref[edge * 7:edge * 8, :] = jnp.where(leaving, index_ref[start:start + edge, :].astype(F32), F32(-1.0))


def pack_kernel(slabs, slab_ref, got_ref, head_ref, tail_ref, out_ref):
    moments = got_ref[0]
    for source in range(1, got_ref.shape[0]):
        moments = moments + got_ref[source]
    head, tail = head_ref[...], tail_ref[...]
    for slab in range(slabs):
        out_ref[slab] = jnp.where(slab < slab_ref[0], head, tail)
        out_ref[slab, 0:3, :] = moments[0:3]


def finish_kernel(slabs, local, capacity, slab_ref, moving_ref, got_ref, dense_ref, index_ref, near_ref, far_ref, trans_ref, long_ref,
                  hop_ref, coef_ref, kick_ref, out_ref, work_ref, done_ref):
    tiles = local // LANES
    edge = capacity // LANES
    slab = slab_ref[0]
    nt = (((1,), (1,)), ((), ()))
    moments = jnp.concatenate([got_ref[:, c, :] for c in range(3)], axis=0)
    sum_re = lax.dot_general(moments, far_ref[0:8, :], nt, precision=HIGH, preferred_element_type=F32)
    sum_im = lax.dot_general(moments, far_ref[8:16, :], nt, precision=HIGH, preferred_element_type=F32)
    line = lax.broadcasted_iota(jnp.int32, (ROWS, MODES), 0)
    carry_re = jnp.zeros((ROWS, MODES), F32)
    carry_im = jnp.zeros((ROWS, MODES), F32)
    for index in range(3):
        weight = hop_ref[2 * index], hop_ref[2 * index + 1]
        for c in range(3):
            part = complex_mul(weight, (sum_re[c * slabs:(c + 1) * slabs], sum_im[c * slabs:(c + 1) * slabs]))
            part = complex_mul(part, (coef_ref[0], coef_ref[1]) if c < 2 else (coef_ref[2], coef_ref[3]))
            here = line == 8 * index + c
            carry_re = jnp.where(here, jnp.sum(part[0], axis=0, keepdims=True), carry_re)
            carry_im = jnp.where(here, jnp.sum(part[1], axis=0, keepdims=True), carry_im)
    plain = (((1,), (0,)), ((), ()))
    incoming = lax.dot_general(carry_re, near_ref[0:8, :], plain, precision=HIGH, preferred_element_type=F32) - lax.dot_general(
        carry_im, near_ref[8:16, :], plain, precision=HIGH, preferred_element_type=F32)
    ahead = jnp.maximum(slab - 1, 0)
    behind = jnp.minimum(slab + 1, slabs - 1)
    near_moments = jnp.concatenate([got_ref[ahead, 0:8, :], got_ref[slab, 0:8, :], got_ref[behind, 0:8, :]], axis=0)
    by_trans = lax.dot_general(near_moments, trans_ref[...], plain, precision=HIGH, preferred_element_type=F32)
    by_long = lax.dot_general(near_moments, long_ref[...], plain, precision=HIGH, preferred_element_type=F32)
    wide = lax.broadcasted_iota(jnp.int32, (ROWS, LANES), 0)
    kicks = jnp.where(wide % 8 == 2, by_long, by_trans) + incoming
    kick_ref[...] = kicks[8:11]

    for q in range(6):
        work_ref[q * ROWS:q * ROWS + edge, :] = got_ref[behind, edge * (q + 1):edge * (q + 2), :]
        work_ref[q * ROWS + edge:q * ROWS + edge + tiles, :] = dense_ref[q * tiles:(q + 1) * tiles, :]
        work_ref[q * ROWS + edge + tiles:q * ROWS + 2 * edge + tiles, :] = got_ref[ahead, edge * (q + 1):edge * (q + 2), :]
        work_ref[q * ROWS + 2 * edge + tiles:(q + 1) * ROWS, :] = jnp.zeros((ROWS - 2 * edge - tiles, LANES), F32)
    base = 6 * ROWS
    own = (tiles, LANES)
    place = lax.broadcasted_iota(jnp.int32, own, 0) * LANES + lax.broadcasted_iota(jnp.int32, own, 1)
    stays = (place >= moving_ref[0, 0, 0]) & (place < local - moving_ref[0, 0, 1])
    none = F32(-1.0)
    work_ref[base:base + edge, :] = jnp.where(slab < slabs - 1, got_ref[behind, 7 * edge:8 * edge, :], none)
    work_ref[base + edge:base + edge + tiles, :] = jnp.where(stays, index_ref[...].astype(F32), none)
    work_ref[base + edge + tiles:base + 2 * edge + tiles, :] = jnp.where(slab > 0, got_ref[ahead, 7 * edge:8 * edge, :], none)
    work_ref[base + 2 * edge + tiles:base + ROWS, :] = jnp.full((ROWS - 2 * edge - tiles, LANES), -1.0, F32)

    marks = work_ref[base:base + ROWS, :]
    kept = marks >= 0.0
    index = jnp.maximum(marks, 0.0).astype(jnp.int32)

    def kick_of(c):
        table = jnp.where(wide < edge, kicks[16 + c:17 + c], jnp.where(wide < edge + tiles, kicks[8 + c:9 + c], kicks[c:c + 1]))
        return jnp.take_along_axis(table, index, axis=1)

    x, px, y, py, s, e = [work_ref[q * ROWS:(q + 1) * ROWS, :] for q in range(6)]
    px = px + kick_of(0)
    py = py + kick_of(1)
    e = e + kick_of(2)
    jx = 0.5 * (x * x + px * px)
    jy = 0.5 * (y * y + py * py)
    ux = turn_reduce(0.269 + 0.05 * e + 0.02 * e * e + 0.03 * jx - 0.02 * jy)
    uy = turn_reduce(0.355 + 0.04 * e - 0.015 * e * e + 0.03 * jy - 0.02 * jx)
    cx, sx, cy, sy = cosine(ux), sine(ux), cosine(uy), sine(uy)
    e_new = e - 0.05 * (sine(radians_to_turns(0.3 + s)) - F32(math.sin(0.3)))
    s_new = s - 0.1 * e_new
    results = (cx * x + sx * px, cx * px - sx * x, cy * y + sy * py, cy * py - sy * y, s_new, e_new)
    for q, value in enumerate(results):
        done_ref[q * ROWS:(q + 1) * ROWS, :] = jnp.where(kept, value, F32(0.0))
    for tile in range(tiles + 2 * edge):
        out_ref[:, tile * LANES:(tile + 1) * LANES] = done_ref[pl.ds(tile, 6, stride=ROWS), :]


def specs(*kinds):
    return [pl.BlockSpec(memory_space=pltpu.SMEM if kind == "s" else pltpu.VMEM) for kind in kinds]


def shape_of(*dims):
    return jax.ShapeDtypeStruct(dims, F32)


def body(particles, slice_index, moving, decay_rate, wake_freq, wake_amp):
    slabs = lax.axis_size("gz")
    members = lax.axis_size("pa")
    local = particles.shape[1]
    capacity = local * 3 // 16
    tiles = local // LANES
    fill = local * members / LANES
    slab = lax.axis_index("gz").astype(jnp.int32).reshape(1)
    index = slice_index.reshape(tiles, LANES)

    near, far, trans, long, hop, coef = pl.pallas_call(
        functools.partial(tables_kernel, slabs, LANES),
        out_shape=[shape_of(16, LANES), shape_of(16, LANES), shape_of(LANES, LANES), shape_of(LANES, LANES),
                   shape_of(6, slabs, MODES), shape_of(4, slabs, MODES)],
        in_specs=specs(*"ssss"),
        out_specs=specs(*"vvvvvv"),
        name="tables",
    )(slab, decay_rate, wake_freq, wake_amp)

    moments, dense, head, tail = pl.pallas_call(
        functools.partial(deposit_kernel, local, capacity, fill),
        out_shape=[shape_of(4, LANES), shape_of(6 * tiles, LANES), shape_of(ROWS, LANES), shape_of(ROWS, LANES)],
        in_specs=specs(*"vvs"),
        out_specs=specs(*"vvvv"),
        name="deposit",
    )(particles, index, moving)

    chips = members // 2
    pairs = [[2 * z, 2 * z + 1] for z in range(chips)]
    rings = [[2 * z + core for z in range(chips)] for core in range(2)]
    both = lax.all_gather(moments, "pa", axis_index_groups=pairs)
    spread_out = jnp.broadcast_to(both[0] + both[1], (chips, 4, LANES))
    gathered = lax.all_to_all(spread_out, "pa", 0, 0, axis_index_groups=rings)
    packed = pl.pallas_call(
        functools.partial(pack_kernel, slabs),
        out_shape=shape_of(slabs, ROWS, LANES),
        in_specs=specs(*"svvv"),
        out_specs=specs("v")[0],
        name="pack",
    )(slab, gathered, head, tail)
    everyone = lax.all_to_all(packed, "gz", 0, 0)
    return pl.pallas_call(
        functools.partial(finish_kernel, slabs, local, capacity),
        out_shape=[shape_of(3, LANES), shape_of(6, local + 2 * capacity)],
        in_specs=specs(*"ssvvvvvvvvv"),
        out_specs=specs(*"vv"),
        scratch_shapes=[pltpu.VMEM((7 * ROWS, LANES), F32), pltpu.VMEM((6 * ROWS, LANES), F32)],
        name="finish",
    )(slab, moving, everyone, dense, index, near, far, trans, long, hop, coef)


def solution(mesh):
    return jax.shard_map(
        body,
        mesh=mesh,
        in_specs=(P(None, ("gz", "pa")), P(("gz", "pa")), P("gz", "pa", None), P(), P(), P()),
        out_specs=(P(None, "gz"), P(None, ("gz", "pa"))),
        check_vma=False,
    )
```

```python
import functools
import math

import jax
import jax.numpy as jnp
from jax import lax
from jax.experimental import pallas as pl
from jax.experimental.pallas import tpu as pltpu
from jax.sharding import PartitionSpec as P

LANES = 128
MODES = 8
ROWS = 24
HIGH = lax.Precision.HIGHEST
F32 = jnp.float32

COS_TERMS = (1.0, -19.73920440673828, 64.93911743164062, -85.45014190673828, 60.167633056640625,
             -25.967601776123047, 6.528658866882324)
SIN_TERMS = (6.2831854820251465, -41.34170150756836, 81.60513305664062, -76.70301818847656,
             42.02592849731445, -14.899847984313965, 3.238137722015381)
SMALL = pltpu.CompilerParams(vmem_limit_bytes=4 << 20)
FIRST_RING = 8
FIRST_SLAB = 10
INV_TWO_PI = 0.15915494309189535
TURN_PARTS = (6.28125, 1.93500518798828125e-3, 3.0199159819567529e-7)


def horner(terms, t):
    total = jnp.full_like(t, terms[-1])
    for term in terms[-2::-1]:
        total = total * t + F32(term)
    return total


def turn_reduce(turns):
    return turns - jnp.floor(turns + F32(0.5))


def sine(turns):
    return turns * horner(SIN_TERMS, turns * turns)


def cosine(turns):
    return horner(COS_TERMS, turns * turns)


def radians_to_turns(angle):
    whole = jnp.floor(angle * F32(INV_TWO_PI) + F32(0.5))
    rest = angle
    for part in TURN_PARTS:
        rest = rest - whole * F32(part)
    return rest * F32(INV_TWO_PI)


def powers(damping, freq, distance):
    envelope = jnp.exp(-damping * distance)
    turns = radians_to_turns(freq * distance)
    return envelope * cosine(turns), envelope * sine(turns)


def complex_mul(a, b):
    return a[0] * b[0] - a[1] * b[1], a[0] * b[1] + a[1] * b[0]


def spread(read, shape, axis):
    where = lax.broadcasted_iota(jnp.int32, shape, axis)
    total = jnp.zeros(shape, F32)
    for mode in range(MODES):
        total = jnp.where(where == mode, read(mode), total)
    return total


def make_tables(slabs, width, slab_ref, decay_ref, freq_ref, amp_ref, near_ref, far_ref, trans_ref, long_ref, hop_ref, coef_ref):
    shape = (MODES, LANES)
    scale = F32(1.0 / (slabs * width))
    damping = spread(lambda m: decay_ref[m], shape, 0) * scale
    freq = spread(lambda m: freq_ref[m], shape, 0)
    amps = [spread(functools.partial(lambda row, m: amp_ref[row, m], row), shape, 0) for row in range(4)]
    distance = lax.broadcasted_iota(jnp.int32, shape, 1).astype(F32)
    near = powers(damping, freq, distance)
    far = powers(damping, freq, F32(width) - distance)
    near_ref[0:8, :] = near[0]
    near_ref[8:16, :] = near[1]
    far_ref[0:8, :] = far[0]
    far_ref[8:16, :] = far[1]
    norm_trans = jnp.sqrt(2.0 * damping)
    norm_long = jnp.sqrt(damping * damping + freq * freq)
    wave_trans = jnp.sum(norm_trans * (amps[0] * near[0] - amps[1] * near[1]), axis=0, keepdims=True)
    wave_long = jnp.sum(norm_long * (amps[2] * near[0] - amps[3] * near[1]), axis=0, keepdims=True)
    square = (LANES, LANES)
    later = lax.broadcasted_iota(jnp.int32, square, 1) > lax.broadcasted_iota(jnp.int32, square, 0)
    for wave, ref in ((wave_trans, trans_ref), (wave_long, long_ref)):
        shifted = pltpu.roll(jnp.broadcast_to(wave, square), 0, 1, stride=1, stride_axis=0)
        ref[...] = jnp.where(later, shifted, F32(0.0))

    small = (slabs, MODES)
    damping = spread(lambda m: decay_ref[m], small, 1) * scale
    freq = spread(lambda m: freq_ref[m], small, 1)
    amps = [spread(functools.partial(lambda row, m: amp_ref[row, m], row), small, 1) for row in range(4)]
    norm_trans = jnp.sqrt(2.0 * damping)
    norm_long = jnp.sqrt(damping * damping + freq * freq)
    coef_ref[0] = amps[0] * norm_trans
    coef_ref[1] = amps[1] * norm_trans
    coef_ref[2] = amps[2] * norm_long
    coef_ref[3] = amps[3] * norm_long
    step = powers(damping, freq, jnp.full(small, width, F32))
    ladder = [step]
    while 2 ** len(ladder) < slabs:
        ladder.append(complex_mul(ladder[-1], ladder[-1]))
    source = lax.broadcasted_iota(jnp.int32, small, 0) ^ FIRST_SLAB
    for index in range(3):
        hops = slab_ref[0] + (index - 2) - source
        weight = (jnp.ones(small, F32), jnp.zeros(small, F32))
        for bit, factor in enumerate(ladder):
            longer = complex_mul(weight, factor)
            taken = (hops & (1 << bit)) != 0
            weight = tuple(jnp.where(taken, b, a) for a, b in zip(weight, longer))
        ahead = hops >= 0
        hop_ref[2 * index] = jnp.where(ahead, weight[0], F32(0.0))
        hop_ref[2 * index + 1] = jnp.where(ahead, weight[1], F32(0.0))


def fetch(sources, targets, sems):
    copies = [pltpu.make_async_copy(a, b, sems.at[k]) for k, (a, b) in enumerate(zip(sources, targets))]
    for copy in copies:
        copy.start()
    for copy in copies:
        copy.wait()


def deposit_kernel(local, fill, part_hbm, index_hbm, moment_ref, part_ref, index_ref, sems):
    tiles = local // LANES
    fetch((part_hbm, index_hbm), (part_ref, index_ref), sems)
    shape = (8, local)
    row = lax.broadcasted_iota(jnp.int32, shape, 0)
    base = jnp.where(row < 3, part_ref[0:1, :], jnp.where(row < 6, part_ref[2:3, :], F32(1.0)))
    bf = jnp.bfloat16
    high = base.astype(bf).astype(F32)
    rest = base - high
    mid = rest.astype(bf).astype(F32)
    low = rest - mid
    third = row % 3
    values = jnp.where(third == 0, high, jnp.where(third == 1, mid, low)).astype(bf)
    slot = lax.broadcasted_iota(jnp.int32, (LANES, LANES), 0)
    total = jnp.zeros((8, LANES), F32)
    group = 2
    for first in range(0, tiles, group):
        hot = jnp.concatenate(
            [(slot == index_ref[t:t + 1, :]).astype(F32).astype(bf) for t in range(first, first + group)], axis=1
        )
        total = total + lax.dot_general(
            values[:, first * LANES:(first + group) * LANES], hot, (((1,), (1,)), ((), ())), preferred_element_type=F32
        )
    root = F32(1.0 / math.sqrt(fill))
    moment_ref[0:1, :] = (total[0:1] + total[1:2] + total[2:3]) * root
    moment_ref[1:2, :] = (total[3:4] + total[4:5] + total[5:6]) * root
    moment_ref[2:3, :] = total[6:7] * F32(1.0 / fill)
    moment_ref[3:4, :] = jnp.zeros((1, LANES), F32)


def make_payload(local, capacity, part_ref, index_ref, moving_ref, dense_ref, head_ref, tail_ref):
    tiles = local // LANES
    for tile in range(tiles):
        dense_ref[pl.ds(tile, 6, stride=tiles), :] = part_ref[:, tile * LANES:(tile + 1) * LANES]
    edge = capacity // LANES
    place = lax.broadcasted_iota(jnp.int32, (edge, LANES), 0) * LANES + lax.broadcasted_iota(jnp.int32, (edge, LANES), 1)
    for ref, start, leaving in (
        (head_ref, 0, place < moving_ref[0, 0, 0]),
        (tail_ref, tiles - edge, place >= capacity - moving_ref[0, 0, 1]),
    ):
        ref[0:edge, :] = jnp.zeros((edge, LANES), F32)
        for q in range(6):
            ref[edge * (q + 1):edge * (q + 2), :] = dense_ref[q * tiles + start:q * tiles + start + edge, :]
        ref[edge * 7:edge * 8, :] = jnp.where(leaving, index_ref[start:start + edge, :].astype(F32), F32(-1.0))


def prepare_kernel(slabs, local, capacity, slab_ref, part_hbm, index_hbm, moving_hbm, decay_hbm, freq_hbm, amp_hbm, *refs):
    outs, (part_ref, index_ref, moving_ref, decay_ref, freq_ref, amp_ref, sems) = refs[:9], refs[9:]
    fetch((part_hbm, index_hbm, moving_hbm, decay_hbm, freq_hbm, amp_hbm),
          (part_ref, index_ref, moving_ref, decay_ref, freq_ref, amp_ref), sems)
    make_payload(local, capacity, part_ref, index_ref, moving_ref, *outs[:3])
    make_tables(slabs, LANES, slab_ref, decay_ref, freq_ref, amp_ref, *outs[3:])


def repeat_kernel(both_ref, out_ref):
    total = both_ref[0] + both_ref[1]
    for slot in range(out_ref.shape[0]):
        out_ref[slot] = total


def pack_kernel(slabs, slab_ref, got_ref, head_ref, tail_ref, out_ref):
    moments = got_ref[0]
    for source in range(1, got_ref.shape[0]):
        moments = moments + got_ref[source]
    head, tail = head_ref[...], tail_ref[...]
    for slot in range(slabs):
        out_ref[slot] = jnp.where((slot ^ FIRST_SLAB) < slab_ref[0], head, tail)
        out_ref[slot, 0:3, :] = moments[0:3]


def finish_kernel(slabs, local, capacity, slab_ref, moving_ref, got_ref, dense_ref, index_ref, near_ref, far_ref, trans_ref, long_ref,
                  hop_ref, coef_ref, kick_ref, out_ref, work_ref, done_ref):
    tiles = local // LANES
    edge = capacity // LANES
    slab = slab_ref[0]
    nt = (((1,), (1,)), ((), ()))
    moments = jnp.concatenate([got_ref[:, c, :] for c in range(3)], axis=0)
    sum_re = lax.dot_general(moments, far_ref[0:8, :], nt, precision=HIGH, preferred_element_type=F32)
    sum_im = lax.dot_general(moments, far_ref[8:16, :], nt, precision=HIGH, preferred_element_type=F32)
    line = lax.broadcasted_iota(jnp.int32, (ROWS, MODES), 0)
    carry_re = jnp.zeros((ROWS, MODES), F32)
    carry_im = jnp.zeros((ROWS, MODES), F32)
    for index in range(3):
        weight = hop_ref[2 * index], hop_ref[2 * index + 1]
        for c in range(3):
            part = complex_mul(weight, (sum_re[c * slabs:(c + 1) * slabs], sum_im[c * slabs:(c + 1) * slabs]))
            part = complex_mul(part, (coef_ref[0], coef_ref[1]) if c < 2 else (coef_ref[2], coef_ref[3]))
            here = line == 8 * index + c
            carry_re = jnp.where(here, jnp.sum(part[0], axis=0, keepdims=True), carry_re)
            carry_im = jnp.where(here, jnp.sum(part[1], axis=0, keepdims=True), carry_im)
    plain = (((1,), (0,)), ((), ()))
    incoming = lax.dot_general(carry_re, near_ref[0:8, :], plain, precision=HIGH, preferred_element_type=F32) - lax.dot_general(
        carry_im, near_ref[8:16, :], plain, precision=HIGH, preferred_element_type=F32)
    ahead = jnp.maximum(slab - 1, 0) ^ FIRST_SLAB
    behind = jnp.minimum(slab + 1, slabs - 1) ^ FIRST_SLAB
    near_moments = jnp.concatenate([got_ref[ahead, 0:8, :], got_ref[slab ^ FIRST_SLAB, 0:8, :], got_ref[behind, 0:8, :]], axis=0)
    by_trans = lax.dot_general(near_moments, trans_ref[...], plain, precision=HIGH, preferred_element_type=F32)
    by_long = lax.dot_general(near_moments, long_ref[...], plain, precision=HIGH, preferred_element_type=F32)
    wide = lax.broadcasted_iota(jnp.int32, (ROWS, LANES), 0)
    kicks = jnp.where(wide % 8 == 2, by_long, by_trans) + incoming
    kick_ref[...] = kicks[8:11]

    for q in range(6):
        work_ref[q * ROWS:q * ROWS + edge, :] = got_ref[behind, edge * (q + 1):edge * (q + 2), :]
        work_ref[q * ROWS + edge:q * ROWS + edge + tiles, :] = dense_ref[q * tiles:(q + 1) * tiles, :]
        work_ref[q * ROWS + edge + tiles:q * ROWS + 2 * edge + tiles, :] = got_ref[ahead, edge * (q + 1):edge * (q + 2), :]
        work_ref[q * ROWS + 2 * edge + tiles:(q + 1) * ROWS, :] = jnp.zeros((ROWS - 2 * edge - tiles, LANES), F32)
    base = 6 * ROWS
    own = (tiles, LANES)
    place = lax.broadcasted_iota(jnp.int32, own, 0) * LANES + lax.broadcasted_iota(jnp.int32, own, 1)
    stays = (place >= moving_ref[0, 0, 0]) & (place < local - moving_ref[0, 0, 1])
    none = F32(-1.0)
    work_ref[base:base + edge, :] = jnp.where(slab < slabs - 1, got_ref[behind, 7 * edge:8 * edge, :], none)
    work_ref[base + edge:base + edge + tiles, :] = jnp.where(stays, index_ref[...].astype(F32), none)
    work_ref[base + edge + tiles:base + 2 * edge + tiles, :] = jnp.where(slab > 0, got_ref[ahead, 7 * edge:8 * edge, :], none)
    work_ref[base + 2 * edge + tiles:base + ROWS, :] = jnp.full((ROWS - 2 * edge - tiles, LANES), -1.0, F32)

    marks = work_ref[base:base + ROWS, :]
    kept = marks >= 0.0
    index = jnp.maximum(marks, 0.0).astype(jnp.int32)

    def kick_of(c):
        table = jnp.where(wide < edge, kicks[16 + c:17 + c], jnp.where(wide < edge + tiles, kicks[8 + c:9 + c], kicks[c:c + 1]))
        return jnp.take_along_axis(table, index, axis=1)

    x, px, y, py, s, e = [work_ref[q * ROWS:(q + 1) * ROWS, :] for q in range(6)]
    px = px + kick_of(0)
    py = py + kick_of(1)
    e = e + kick_of(2)
    jx = 0.5 * (x * x + px * px)
    jy = 0.5 * (y * y + py * py)
    ux = turn_reduce(0.269 + 0.05 * e + 0.02 * e * e + 0.03 * jx - 0.02 * jy)
    uy = turn_reduce(0.355 + 0.04 * e - 0.015 * e * e + 0.03 * jy - 0.02 * jx)
    cx, sx, cy, sy = cosine(ux), sine(ux), cosine(uy), sine(uy)
    e_new = e - 0.05 * (sine(radians_to_turns(0.3 + s)) - F32(math.sin(0.3)))
    s_new = s - 0.1 * e_new
    results = (cx * x + sx * px, cx * px - sx * x, cy * y + sy * py, cy * py - sy * y, s_new, e_new)
    for q, value in enumerate(results):
        done_ref[q * ROWS:(q + 1) * ROWS, :] = jnp.where(kept, value, F32(0.0))
    for tile in range(tiles + 2 * edge):
        out_ref[:, tile * LANES:(tile + 1) * LANES] = done_ref[pl.ds(tile, 6, stride=ROWS), :]


def specs(*kinds):
    return [pl.BlockSpec(memory_space={"s": pltpu.SMEM, "v": pltpu.VMEM, "h": pltpu.HBM}[kind]) for kind in kinds]


def stay(array):
    return pltpu.with_memory_space_constraint(array, pltpu.HBM)


def shape_of(*dims):
    return jax.ShapeDtypeStruct(dims, F32)


def body(particles, slice_index, moving, decay_rate, wake_freq, wake_amp):
    slabs = lax.axis_size("gz")
    members = lax.axis_size("pa")
    local = particles.shape[1]
    capacity = local * 3 // 16
    tiles = local // LANES
    fill = local * members / LANES
    slab = lax.axis_index("gz").astype(jnp.int32).reshape(1)
    index = slice_index.reshape(tiles, LANES)

    moments = pl.pallas_call(
        functools.partial(deposit_kernel, local, fill),
        out_shape=shape_of(4, LANES),
        in_specs=specs(*"hh"),
        out_specs=specs("v")[0],
        scratch_shapes=[pltpu.VMEM((6, local), F32), pltpu.VMEM((tiles, LANES), jnp.int32), pltpu.SemaphoreType.DMA((2,))],
        compiler_params=SMALL,
        name="deposit",
    )(stay(particles), stay(index))
    dense, head, tail, near, far, trans, long, hop, coef = pl.pallas_call(
        functools.partial(prepare_kernel, slabs, local, capacity),
        out_shape=[shape_of(6 * tiles, LANES), shape_of(ROWS, LANES), shape_of(ROWS, LANES),
                   shape_of(16, LANES), shape_of(16, LANES), shape_of(LANES, LANES), shape_of(LANES, LANES),
                   shape_of(6, slabs, MODES), shape_of(4, slabs, MODES)],
        in_specs=specs(*"shhhhhh"),
        out_specs=specs(*"vvvvvvvvv"),
        scratch_shapes=[pltpu.VMEM((6, local), F32), pltpu.VMEM((tiles, LANES), jnp.int32), pltpu.SMEM((1, 1, 2), jnp.int32),
                        pltpu.SMEM((MODES,), F32), pltpu.SMEM((MODES,), F32), pltpu.SMEM((4, MODES), F32),
                        pltpu.SemaphoreType.DMA((6,))],
        compiler_params=SMALL,
        name="prepare",
    )(slab, *[stay(array) for array in (particles, index, moving, decay_rate, wake_freq, wake_amp)])

    chips = members // 2
    pairs = [[2 * z + 1, 2 * z] for z in range(chips)]
    rings = [[2 * ((z + FIRST_RING) % chips) + core for z in range(chips)] for core in range(2)]
    order = [slot ^ FIRST_SLAB for slot in range(slabs)]
    both = lax.all_gather(moments, "pa", axis_index_groups=pairs)
    repeated = pl.pallas_call(
        repeat_kernel,
        out_shape=pltpu.VMEM((chips, 4, LANES), F32),
        in_specs=specs("v"),
        out_specs=specs("v")[0],
        compiler_params=SMALL,
        name="repeat",
    )(both)
    gathered = lax.all_to_all(repeated, "pa", 0, 0, axis_index_groups=rings)
    gathered, dense, head, tail, near, far, trans, long, hop, coef = lax.optimization_barrier(
        (gathered, dense, head, tail, near, far, trans, long, hop, coef)
    )
    packed = pl.pallas_call(
        functools.partial(pack_kernel, slabs),
        out_shape=pltpu.VMEM((slabs, ROWS, LANES), F32),
        in_specs=specs(*"svvv"),
        out_specs=specs("v")[0],
        compiler_params=SMALL,
        name="pack",
    )(slab, gathered, head, tail)
    everyone = lax.all_to_all(packed, "gz", 0, 0, axis_index_groups=[order])
    return pl.pallas_call(
        functools.partial(finish_kernel, slabs, local, capacity),
        out_shape=[shape_of(3, LANES), shape_of(6, local + 2 * capacity)],
        in_specs=specs(*"ssvvvvvvvvv"),
        out_specs=specs(*"vv"),
        scratch_shapes=[pltpu.VMEM((7 * ROWS, LANES), F32), pltpu.VMEM((6 * ROWS, LANES), F32)],
        compiler_params=SMALL,
        name="finish",
    )(slab, moving, everyone, dense, index, near, far, trans, long, hop, coef)


def solution(mesh):
    return jax.shard_map(
        body,
        mesh=mesh,
        in_specs=(P(None, ("gz", "pa")), P(("gz", "pa")), P("gz", "pa", None), P(), P(), P()),
        out_specs=(P(None, "gz"), P(None, ("gz", "pa"))),
        check_vma=False,
    )
```

```python
import functools
import math

import jax
import jax.numpy as jnp
from jax import lax
from jax.experimental import pallas as pl
from jax.experimental.pallas import tpu as pltpu
from jax.sharding import PartitionSpec as P

LANES = 128
MODES = 8
ROWS = 24
HIGH = lax.Precision.HIGHEST
F32 = jnp.float32

COS_TERMS = (1.0, -19.73920440673828, 64.93911743164062, -85.45014190673828, 60.167633056640625,
             -25.967601776123047, 6.528658866882324)
SIN_TERMS = (6.2831854820251465, -41.34170150756836, 81.60513305664062, -76.70301818847656,
             42.02592849731445, -14.899847984313965, 3.238137722015381)
SMALL = pltpu.CompilerParams(vmem_limit_bytes=4 << 20)
FIRST_RING = 8
FIRST_SLAB = 10
INV_TWO_PI = 0.15915494309189535
TURN_PARTS = (6.28125, 1.93500518798828125e-3, 3.0199159819567529e-7)


def horner(terms, t):
    total = jnp.full_like(t, terms[-1])
    for term in terms[-2::-1]:
        total = total * t + F32(term)
    return total


def turn_reduce(turns):
    return turns - jnp.floor(turns + F32(0.5))


def sine(turns):
    return turns * horner(SIN_TERMS, turns * turns)


def cosine(turns):
    return horner(COS_TERMS, turns * turns)


def radians_to_turns(angle):
    whole = jnp.floor(angle * F32(INV_TWO_PI) + F32(0.5))
    rest = angle
    for part in TURN_PARTS:
        rest = rest - whole * F32(part)
    return rest * F32(INV_TWO_PI)


def powers(damping, freq, distance):
    envelope = jnp.exp(-damping * distance)
    turns = radians_to_turns(freq * distance)
    return envelope * cosine(turns), envelope * sine(turns)


def complex_mul(a, b):
    return a[0] * b[0] - a[1] * b[1], a[0] * b[1] + a[1] * b[0]


def spread(read, shape, axis):
    where = lax.broadcasted_iota(jnp.int32, shape, axis)
    total = jnp.zeros(shape, F32)
    for mode in range(MODES):
        total = jnp.where(where == mode, read(mode), total)
    return total


def make_tables(slabs, width, slab_ref, decay_ref, freq_ref, amp_ref, near_ref, far_ref, trans_ref, long_ref, hop_ref, coef_ref):
    shape = (MODES, LANES)
    scale = F32(1.0 / (slabs * width))
    damping = spread(lambda m: decay_ref[m], shape, 0) * scale
    freq = spread(lambda m: freq_ref[m], shape, 0)
    amps = [spread(functools.partial(lambda row, m: amp_ref[row, m], row), shape, 0) for row in range(4)]
    distance = lax.broadcasted_iota(jnp.int32, shape, 1).astype(F32)
    near = powers(damping, freq, distance)
    far = powers(damping, freq, F32(width) - distance)
    near_ref[0:8, :] = near[0]
    near_ref[8:16, :] = near[1]
    far_ref[0:8, :] = far[0]
    far_ref[8:16, :] = far[1]
    norm_trans = jnp.sqrt(2.0 * damping)
    norm_long = jnp.sqrt(damping * damping + freq * freq)
    wave_trans = jnp.sum(norm_trans * (amps[0] * near[0] - amps[1] * near[1]), axis=0, keepdims=True)
    wave_long = jnp.sum(norm_long * (amps[2] * near[0] - amps[3] * near[1]), axis=0, keepdims=True)
    square = (LANES, LANES)
    later = lax.broadcasted_iota(jnp.int32, square, 1) > lax.broadcasted_iota(jnp.int32, square, 0)
    for wave, ref in ((wave_trans, trans_ref), (wave_long, long_ref)):
        shifted = pltpu.roll(jnp.broadcast_to(wave, square), 0, 1, stride=1, stride_axis=0)
        ref[...] = jnp.where(later, shifted, F32(0.0))

    small = (slabs, MODES)
    damping = spread(lambda m: decay_ref[m], small, 1) * scale
    freq = spread(lambda m: freq_ref[m], small, 1)
    amps = [spread(functools.partial(lambda row, m: amp_ref[row, m], row), small, 1) for row in range(4)]
    norm_trans = jnp.sqrt(2.0 * damping)
    norm_long = jnp.sqrt(damping * damping + freq * freq)
    coef_ref[0] = amps[0] * norm_trans
    coef_ref[1] = amps[1] * norm_trans
    coef_ref[2] = amps[2] * norm_long
    coef_ref[3] = amps[3] * norm_long
    step = powers(damping, freq, jnp.full(small, width, F32))
    ladder = [step]
    while 2 ** len(ladder) < slabs:
        ladder.append(complex_mul(ladder[-1], ladder[-1]))
    source = lax.broadcasted_iota(jnp.int32, small, 0) ^ FIRST_SLAB
    for index in range(3):
        hops = slab_ref[0] + (index - 2) - source
        weight = (jnp.ones(small, F32), jnp.zeros(small, F32))
        for bit, factor in enumerate(ladder):
            longer = complex_mul(weight, factor)
            taken = (hops & (1 << bit)) != 0
            weight = tuple(jnp.where(taken, b, a) for a, b in zip(weight, longer))
        ahead = hops >= 0
        hop_ref[2 * index] = jnp.where(ahead, weight[0], F32(0.0))
        hop_ref[2 * index + 1] = jnp.where(ahead, weight[1], F32(0.0))


def fetch(sources, targets, sems):
    copies = [pltpu.make_async_copy(a, b, sems.at[k]) for k, (a, b) in enumerate(zip(sources, targets))]
    for copy in copies:
        copy.start()
    for copy in copies:
        copy.wait()


def deposit(local, fill, part_ref, index_ref, moment_ref):
    tiles = local // LANES
    shape = (8, local)
    row = lax.broadcasted_iota(jnp.int32, shape, 0)
    base = jnp.where(row < 3, part_ref[0:1, :], jnp.where(row < 6, part_ref[2:3, :], F32(1.0)))
    bf = jnp.bfloat16
    high = base.astype(bf).astype(F32)
    rest = base - high
    mid = rest.astype(bf).astype(F32)
    low = rest - mid
    third = row % 3
    values = jnp.where(third == 0, high, jnp.where(third == 1, mid, low)).astype(bf)
    slot = lax.broadcasted_iota(jnp.int32, (LANES, LANES), 0)
    total = jnp.zeros((8, LANES), F32)
    group = 2
    for first in range(0, tiles, group):
        hot = jnp.concatenate(
            [(slot == index_ref[t:t + 1, :]).astype(F32).astype(bf) for t in range(first, first + group)], axis=1
        )
        total = total + lax.dot_general(
            values[:, first * LANES:(first + group) * LANES], hot, (((1,), (1,)), ((), ())), preferred_element_type=F32
        )
    root = F32(1.0 / math.sqrt(fill))
    moment_ref[0:1, :] = (total[0:1] + total[1:2] + total[2:3]) * root
    moment_ref[1:2, :] = (total[3:4] + total[4:5] + total[5:6]) * root
    moment_ref[2:3, :] = total[6:7] * F32(1.0 / fill)
    moment_ref[3:4, :] = jnp.zeros((1, LANES), F32)


def make_payload(local, capacity, part_ref, index_ref, moving_ref, dense_ref, head_ref, tail_ref):
    tiles = local // LANES
    for tile in range(tiles):
        dense_ref[pl.ds(tile, 6, stride=tiles), :] = part_ref[:, tile * LANES:(tile + 1) * LANES]
    own = (tiles, LANES)
    position = lax.broadcasted_iota(jnp.int32, own, 0) * LANES + lax.broadcasted_iota(jnp.int32, own, 1)
    stays = (position >= moving_ref[0, 0, 0]) & (position < local - moving_ref[0, 0, 1])
    dense_ref[6 * tiles:7 * tiles, :] = jnp.where(stays, index_ref[...].astype(F32), F32(-1.0))
    edge = capacity // LANES
    place = lax.broadcasted_iota(jnp.int32, (edge, LANES), 0) * LANES + lax.broadcasted_iota(jnp.int32, (edge, LANES), 1)
    for ref, start, leaving in (
        (head_ref, 0, place < moving_ref[0, 0, 0]),
        (tail_ref, tiles - edge, place >= capacity - moving_ref[0, 0, 1]),
    ):
        ref[0:edge, :] = jnp.zeros((edge, LANES), F32)
        for q in range(6):
            ref[edge * (q + 1):edge * (q + 2), :] = dense_ref[q * tiles + start:q * tiles + start + edge, :]
        ref[edge * 7:edge * 8, :] = jnp.where(leaving, index_ref[start:start + edge, :].astype(F32), F32(-1.0))


def deposit_kernel(slabs, local, capacity, fill, slab_ref, part_hbm, index_hbm, moving_hbm, decay_hbm, freq_hbm, amp_hbm, *refs):
    outs, (part_ref, index_ref, moving_ref, decay_ref, freq_ref, amp_ref, sems) = refs[:10], refs[10:]
    fetch((part_hbm, index_hbm, moving_hbm, decay_hbm, freq_hbm, amp_hbm),
          (part_ref, index_ref, moving_ref, decay_ref, freq_ref, amp_ref), sems)
    deposit(local, fill, part_ref, index_ref, outs[0])
    make_payload(local, capacity, part_ref, index_ref, moving_ref, *outs[1:4])
    make_tables(slabs, LANES, slab_ref, decay_ref, freq_ref, amp_ref, *outs[4:])


def repeat_kernel(both_ref, out_ref):
    total = both_ref[0] + both_ref[1]
    for slot in range(out_ref.shape[0]):
        out_ref[slot] = total


def pack_kernel(slabs, slab_ref, got_ref, head_ref, tail_ref, out_ref):
    moments = got_ref[0]
    for source in range(1, got_ref.shape[0]):
        moments = moments + got_ref[source]
    head, tail = head_ref[...], tail_ref[...]
    for slot in range(slabs):
        out_ref[slot] = jnp.where((slot ^ FIRST_SLAB) < slab_ref[0], head, tail)
        out_ref[slot, 0:3, :] = moments[0:3]


def finish_kernel(slabs, local, capacity, slab_ref, got_ref, dense_ref, near_ref, far_ref, trans_ref, long_ref,
                  hop_ref, coef_ref, kick_ref, out_ref, work_ref, done_ref):
    tiles = local // LANES
    edge = capacity // LANES
    slab = slab_ref[0]
    nt = (((1,), (1,)), ((), ()))
    moments = jnp.concatenate([got_ref[:, c, :] for c in range(3)], axis=0)
    sum_re = lax.dot_general(moments, far_ref[0:8, :], nt, precision=HIGH, preferred_element_type=F32)
    sum_im = lax.dot_general(moments, far_ref[8:16, :], nt, precision=HIGH, preferred_element_type=F32)
    line = lax.broadcasted_iota(jnp.int32, (ROWS, MODES), 0)
    carry_re = jnp.zeros((ROWS, MODES), F32)
    carry_im = jnp.zeros((ROWS, MODES), F32)
    for index in range(3):
        weight = hop_ref[2 * index], hop_ref[2 * index + 1]
        for c in range(3):
            part = complex_mul(weight, (sum_re[c * slabs:(c + 1) * slabs], sum_im[c * slabs:(c + 1) * slabs]))
            part = complex_mul(part, (coef_ref[0], coef_ref[1]) if c < 2 else (coef_ref[2], coef_ref[3]))
            here = line == 8 * index + c
            carry_re = jnp.where(here, jnp.sum(part[0], axis=0, keepdims=True), carry_re)
            carry_im = jnp.where(here, jnp.sum(part[1], axis=0, keepdims=True), carry_im)
    plain = (((1,), (0,)), ((), ()))
    incoming = lax.dot_general(carry_re, near_ref[0:8, :], plain, precision=HIGH, preferred_element_type=F32) - lax.dot_general(
        carry_im, near_ref[8:16, :], plain, precision=HIGH, preferred_element_type=F32)
    ahead = jnp.maximum(slab - 1, 0) ^ FIRST_SLAB
    behind = jnp.minimum(slab + 1, slabs - 1) ^ FIRST_SLAB
    near_moments = jnp.concatenate([got_ref[ahead, 0:8, :], got_ref[slab ^ FIRST_SLAB, 0:8, :], got_ref[behind, 0:8, :]], axis=0)
    by_trans = lax.dot_general(near_moments, trans_ref[...], plain, precision=HIGH, preferred_element_type=F32)
    by_long = lax.dot_general(near_moments, long_ref[...], plain, precision=HIGH, preferred_element_type=F32)
    wide = lax.broadcasted_iota(jnp.int32, (ROWS, LANES), 0)
    kicks = jnp.where(wide % 8 == 2, by_long, by_trans) + incoming
    kick_ref[...] = kicks[8:11]

    for q in range(6):
        work_ref[q * ROWS:q * ROWS + edge, :] = got_ref[behind, edge * (q + 1):edge * (q + 2), :]
        work_ref[q * ROWS + edge:q * ROWS + edge + tiles, :] = dense_ref[q * tiles:(q + 1) * tiles, :]
        work_ref[q * ROWS + edge + tiles:q * ROWS + 2 * edge + tiles, :] = got_ref[ahead, edge * (q + 1):edge * (q + 2), :]
        work_ref[q * ROWS + 2 * edge + tiles:(q + 1) * ROWS, :] = jnp.zeros((ROWS - 2 * edge - tiles, LANES), F32)
    base = 6 * ROWS
    none = F32(-1.0)
    work_ref[base:base + edge, :] = jnp.where(slab < slabs - 1, got_ref[behind, 7 * edge:8 * edge, :], none)
    work_ref[base + edge:base + edge + tiles, :] = dense_ref[6 * tiles:7 * tiles, :]
    work_ref[base + edge + tiles:base + 2 * edge + tiles, :] = jnp.where(slab > 0, got_ref[ahead, 7 * edge:8 * edge, :], none)
    work_ref[base + 2 * edge + tiles:base + ROWS, :] = jnp.full((ROWS - 2 * edge - tiles, LANES), -1.0, F32)

    marks = work_ref[base:base + ROWS, :]
    kept = marks >= 0.0
    index = jnp.maximum(marks, 0.0).astype(jnp.int32)

    def kick_of(c):
        table = jnp.where(wide < edge, kicks[16 + c:17 + c], jnp.where(wide < edge + tiles, kicks[8 + c:9 + c], kicks[c:c + 1]))
        return jnp.take_along_axis(table, index, axis=1)

    x, px, y, py, s, e = [work_ref[q * ROWS:(q + 1) * ROWS, :] for q in range(6)]
    px = px + kick_of(0)
    py = py + kick_of(1)
    e = e + kick_of(2)
    jx = 0.5 * (x * x + px * px)
    jy = 0.5 * (y * y + py * py)
    ux = turn_reduce(0.269 + 0.05 * e + 0.02 * e * e + 0.03 * jx - 0.02 * jy)
    uy = turn_reduce(0.355 + 0.04 * e - 0.015 * e * e + 0.03 * jy - 0.02 * jx)
    cx, sx, cy, sy = cosine(ux), sine(ux), cosine(uy), sine(uy)
    e_new = e - 0.05 * (sine(radians_to_turns(0.3 + s)) - F32(math.sin(0.3)))
    s_new = s - 0.1 * e_new
    results = (cx * x + sx * px, cx * px - sx * x, cy * y + sy * py, cy * py - sy * y, s_new, e_new)
    for q, value in enumerate(results):
        done_ref[q * ROWS:(q + 1) * ROWS, :] = jnp.where(kept, value, F32(0.0))
    for tile in range(tiles + 2 * edge):
        out_ref[:, tile * LANES:(tile + 1) * LANES] = done_ref[pl.ds(tile, 6, stride=ROWS), :]


def specs(*kinds):
    return [pl.BlockSpec(memory_space={"s": pltpu.SMEM, "v": pltpu.VMEM, "h": pltpu.HBM}[kind]) for kind in kinds]


def stay(array):
    return pltpu.with_memory_space_constraint(array, pltpu.HBM)


def shape_of(*dims):
    return jax.ShapeDtypeStruct(dims, F32)


def body(particles, slice_index, moving, decay_rate, wake_freq, wake_amp):
    slabs = lax.axis_size("gz")
    members = lax.axis_size("pa")
    local = particles.shape[1]
    capacity = local * 3 // 16
    tiles = local // LANES
    fill = local * members / LANES
    slab = lax.axis_index("gz").astype(jnp.int32).reshape(1)
    index = slice_index.reshape(tiles, LANES)

    moments, dense, head, tail, near, far, trans, long, hop, coef = pl.pallas_call(
        functools.partial(deposit_kernel, slabs, local, capacity, fill),
        out_shape=[shape_of(4, LANES), shape_of(7 * tiles, LANES), shape_of(ROWS, LANES), shape_of(ROWS, LANES),
                   shape_of(16, LANES), shape_of(16, LANES), shape_of(LANES, LANES), shape_of(LANES, LANES),
                   shape_of(6, slabs, MODES), shape_of(4, slabs, MODES)],
        in_specs=specs(*"shhhhhh"),
        out_specs=specs(*"vvvvvvvvvv"),
        scratch_shapes=[pltpu.VMEM((6, local), F32), pltpu.VMEM((tiles, LANES), jnp.int32), pltpu.SMEM((1, 1, 2), jnp.int32),
                        pltpu.SMEM((MODES,), F32), pltpu.SMEM((MODES,), F32), pltpu.SMEM((4, MODES), F32),
                        pltpu.SemaphoreType.DMA((6,))],
        compiler_params=SMALL,
        name="deposit",
    )(slab, *[stay(array) for array in (particles, index, moving, decay_rate, wake_freq, wake_amp)])

    chips = members // 2
    pairs = [[2 * z + 1, 2 * z] for z in range(chips)]
    rings = [[2 * ((z + FIRST_RING) % chips) + core for z in range(chips)] for core in range(2)]
    order = [slot ^ FIRST_SLAB for slot in range(slabs)]
    both = lax.all_gather(moments, "pa", axis_index_groups=pairs)
    repeated = pl.pallas_call(
        repeat_kernel,
        out_shape=pltpu.VMEM((chips, 4, LANES), F32),
        in_specs=specs("v"),
        out_specs=specs("v")[0],
        compiler_params=SMALL,
        name="repeat",
    )(both)
    gathered = lax.all_to_all(repeated, "pa", 0, 0, axis_index_groups=rings)
    packed = pl.pallas_call(
        functools.partial(pack_kernel, slabs),
        out_shape=pltpu.VMEM((slabs, ROWS, LANES), F32),
        in_specs=specs(*"svvv"),
        out_specs=specs("v")[0],
        compiler_params=SMALL,
        name="pack",
    )(slab, gathered, head, tail)
    everyone = lax.all_to_all(packed, "gz", 0, 0, axis_index_groups=[order])
    return pl.pallas_call(
        functools.partial(finish_kernel, slabs, local, capacity),
        out_shape=[shape_of(3, LANES), shape_of(6, local + 2 * capacity)],
        in_specs=specs(*"svvvvvvvv"),
        out_specs=specs(*"vv"),
        scratch_shapes=[pltpu.VMEM((7 * ROWS, LANES), F32), pltpu.VMEM((6 * ROWS, LANES), F32)],
        compiler_params=SMALL,
        name="finish",
    )(slab, everyone, dense, near, far, trans, long, hop, coef)


def solution(mesh):
    return jax.shard_map(
        body,
        mesh=mesh,
        in_specs=(P(None, ("gz", "pa")), P(("gz", "pa")), P("gz", "pa", None), P(), P(), P()),
        out_specs=(P(None, "gz"), P(None, ("gz", "pa"))),
        check_vma=False,
    )
```

```python
import functools
import math

import jax
import jax.numpy as jnp
from jax import lax
from jax.experimental import pallas as pl
from jax.experimental.pallas import tpu as pltpu
from jax.sharding import PartitionSpec as P

LANES = 128
MODES = 8
ROWS = 24
HIGH = lax.Precision.HIGHEST
F32 = jnp.float32

COS_TERMS = (1.0, -19.73920440673828, 64.93911743164062, -85.45014190673828, 60.167633056640625,
             -25.967601776123047, 6.528658866882324)
SIN_TERMS = (6.2831854820251465, -41.34170150756836, 81.60513305664062, -76.70301818847656,
             42.02592849731445, -14.899847984313965, 3.238137722015381)
SMALL = pltpu.CompilerParams(vmem_limit_bytes=4 << 20)
FIRST_RING = 8
FIRST_SLAB = 10
INV_TWO_PI = 0.15915494309189535
TURN_PARTS = (6.28125, 1.93500518798828125e-3, 3.0199159819567529e-7)


def horner(terms, t):
    total = jnp.full_like(t, terms[-1])
    for term in terms[-2::-1]:
        total = total * t + F32(term)
    return total


def turn_reduce(turns):
    return turns - jnp.floor(turns + F32(0.5))


def sine(turns):
    return turns * horner(SIN_TERMS, turns * turns)


def cosine(turns):
    return horner(COS_TERMS, turns * turns)


def radians_to_turns(angle):
    whole = jnp.floor(angle * F32(INV_TWO_PI) + F32(0.5))
    rest = angle
    for part in TURN_PARTS:
        rest = rest - whole * F32(part)
    return rest * F32(INV_TWO_PI)


def powers(damping, freq, distance):
    envelope = jnp.exp(-damping * distance)
    turns = radians_to_turns(freq * distance)
    return envelope * cosine(turns), envelope * sine(turns)


def complex_mul(a, b):
    return a[0] * b[0] - a[1] * b[1], a[0] * b[1] + a[1] * b[0]


def spread(read, shape, axis):
    where = lax.broadcasted_iota(jnp.int32, shape, axis)
    total = jnp.zeros(shape, F32)
    for mode in range(MODES):
        total = jnp.where(where == mode, read(mode), total)
    return total


def make_tables(slabs, width, slab_ref, decay_ref, freq_ref, amp_ref, near_ref, far_ref, trans_ref, long_ref, hop_ref, coef_ref):
    shape = (MODES, LANES)
    scale = F32(1.0 / (slabs * width))
    damping = spread(lambda m: decay_ref[m], shape, 0) * scale
    freq = spread(lambda m: freq_ref[m], shape, 0)
    amps = [spread(functools.partial(lambda row, m: amp_ref[row, m], row), shape, 0) for row in range(4)]
    distance = lax.broadcasted_iota(jnp.int32, shape, 1).astype(F32)
    near = powers(damping, freq, distance)
    far = powers(damping, freq, F32(width) - distance)
    near_ref[0:8, :] = near[0]
    near_ref[8:16, :] = near[1]
    far_ref[0:8, :] = far[0]
    far_ref[8:16, :] = far[1]
    norm_trans = jnp.sqrt(2.0 * damping)
    norm_long = jnp.sqrt(damping * damping + freq * freq)
    wave_trans = jnp.sum(norm_trans * (amps[0] * near[0] - amps[1] * near[1]), axis=0, keepdims=True)
    wave_long = jnp.sum(norm_long * (amps[2] * near[0] - amps[3] * near[1]), axis=0, keepdims=True)
    square = (LANES, LANES)
    later = lax.broadcasted_iota(jnp.int32, square, 1) > lax.broadcasted_iota(jnp.int32, square, 0)
    for wave, ref in ((wave_trans, trans_ref), (wave_long, long_ref)):
        shifted = pltpu.roll(jnp.broadcast_to(wave, square), 0, 1, stride=1, stride_axis=0)
        ref[...] = jnp.where(later, shifted, F32(0.0))

    small = (slabs, MODES)
    damping = spread(lambda m: decay_ref[m], small, 1) * scale
    freq = spread(lambda m: freq_ref[m], small, 1)
    amps = [spread(functools.partial(lambda row, m: amp_ref[row, m], row), small, 1) for row in range(4)]
    norm_trans = jnp.sqrt(2.0 * damping)
    norm_long = jnp.sqrt(damping * damping + freq * freq)
    coef_ref[0] = amps[0] * norm_trans
    coef_ref[1] = amps[1] * norm_trans
    coef_ref[2] = amps[2] * norm_long
    coef_ref[3] = amps[3] * norm_long
    step = powers(damping, freq, jnp.full(small, width, F32))
    ladder = [step]
    while 2 ** len(ladder) < slabs:
        ladder.append(complex_mul(ladder[-1], ladder[-1]))
    source = lax.broadcasted_iota(jnp.int32, small, 0) ^ FIRST_SLAB
    for index in range(3):
        hops = slab_ref[0] + (index - 2) - source
        weight = (jnp.ones(small, F32), jnp.zeros(small, F32))
        for bit, factor in enumerate(ladder):
            longer = complex_mul(weight, factor)
            taken = (hops & (1 << bit)) != 0
            weight = tuple(jnp.where(taken, b, a) for a, b in zip(weight, longer))
        ahead = hops >= 0
        hop_ref[2 * index] = jnp.where(ahead, weight[0], F32(0.0))
        hop_ref[2 * index + 1] = jnp.where(ahead, weight[1], F32(0.0))


def fetch(sources, targets, sems):
    copies = [pltpu.make_async_copy(a, b, sems.at[k]) for k, (a, b) in enumerate(zip(sources, targets))]
    for copy in copies:
        copy.start()
    for copy in copies:
        copy.wait()


def deposit(local, fill, part_ref, index_ref, moment_ref):
    tiles = local // LANES
    shape = (8, local)
    row = lax.broadcasted_iota(jnp.int32, shape, 0)
    base = jnp.where(row < 3, part_ref[0:1, :], jnp.where(row < 6, part_ref[2:3, :], F32(1.0)))
    bf = jnp.bfloat16
    high = base.astype(bf).astype(F32)
    rest = base - high
    mid = rest.astype(bf).astype(F32)
    low = rest - mid
    third = row % 3
    values = jnp.where(third == 0, high, jnp.where(third == 1, mid, low)).astype(bf)
    slot = lax.broadcasted_iota(jnp.int32, (LANES, LANES), 0)
    total = jnp.zeros((8, LANES), F32)
    group = 2
    for first in range(0, tiles, group):
        hot = jnp.concatenate(
            [(slot == index_ref[t:t + 1, :]).astype(F32).astype(bf) for t in range(first, first + group)], axis=1
        )
        total = total + lax.dot_general(
            values[:, first * LANES:(first + group) * LANES], hot, (((1,), (1,)), ((), ())), preferred_element_type=F32
        )
    root = F32(1.0 / math.sqrt(fill))
    sums = jnp.concatenate([
        (total[0:1] + total[1:2] + total[2:3]) * root,
        (total[3:4] + total[4:5] + total[5:6]) * root,
        total[6:7] * F32(1.0 / fill),
        jnp.zeros((1, LANES), F32),
    ], axis=0)
    for slot in range(moment_ref.shape[0]):
        for c in range(3):
            moment_ref[slot, :, c * LANES:(c + 1) * LANES] = sums[c:c + 1]


def make_payload(local, capacity, part_ref, index_ref, moving_ref, dense_ref, head_ref, tail_ref):
    tiles = local // LANES
    for tile in range(tiles):
        dense_ref[pl.ds(tile, 6, stride=tiles), :] = part_ref[:, tile * LANES:(tile + 1) * LANES]
    own = (tiles, LANES)
    position = lax.broadcasted_iota(jnp.int32, own, 0) * LANES + lax.broadcasted_iota(jnp.int32, own, 1)
    stays = (position >= moving_ref[0, 0, 0]) & (position < local - moving_ref[0, 0, 1])
    dense_ref[6 * tiles:7 * tiles, :] = jnp.where(stays, index_ref[...].astype(F32), F32(-1.0))
    edge = capacity // LANES
    place = lax.broadcasted_iota(jnp.int32, (edge, LANES), 0) * LANES + lax.broadcasted_iota(jnp.int32, (edge, LANES), 1)
    for ref, start, leaving in (
        (head_ref, 0, place < moving_ref[0, 0, 0]),
        (tail_ref, tiles - edge, place >= capacity - moving_ref[0, 0, 1]),
    ):
        ref[0:edge, :] = jnp.zeros((edge, LANES), F32)
        for q in range(6):
            ref[edge * (q + 1):edge * (q + 2), :] = dense_ref[q * tiles + start:q * tiles + start + edge, :]
        ref[edge * 7:edge * 8, :] = jnp.where(leaving, index_ref[start:start + edge, :].astype(F32), F32(-1.0))


def deposit_kernel(slabs, local, capacity, fill, slab_ref, part_hbm, index_hbm, moving_hbm, decay_hbm, freq_hbm, amp_hbm, *refs):
    outs, (part_ref, index_ref, moving_ref, decay_ref, freq_ref, amp_ref, sems) = refs[:10], refs[10:]
    fetch((part_hbm, index_hbm, moving_hbm, decay_hbm, freq_hbm, amp_hbm),
          (part_ref, index_ref, moving_ref, decay_ref, freq_ref, amp_ref), sems)
    deposit(local, fill, part_ref, index_ref, outs[0])
    make_payload(local, capacity, part_ref, index_ref, moving_ref, *outs[1:4])
    make_tables(slabs, LANES, slab_ref, decay_ref, freq_ref, amp_ref, *outs[4:])


def repeat_kernel(both_ref, out_ref):
    total = both_ref[0] + both_ref[1]
    for slot in range(out_ref.shape[0]):
        out_ref[slot] = total


def pack_kernel(slabs, slab_ref, got_ref, head_ref, tail_ref, out_ref):
    moments = got_ref[0]
    for source in range(1, got_ref.shape[0]):
        moments = moments + got_ref[source]
    head, tail = head_ref[...], tail_ref[...]
    for slot in range(slabs):
        out_ref[slot] = jnp.where((slot ^ FIRST_SLAB) < slab_ref[0], head, tail)
        for c in range(3):
            out_ref[slot, c:c + 1, :] = moments[:, c * LANES:(c + 1) * LANES]


def finish_kernel(slabs, local, capacity, slab_ref, got_ref, dense_ref, near_ref, far_ref, trans_ref, long_ref,
                  hop_ref, coef_ref, kick_ref, out_ref, work_ref, done_ref):
    tiles = local // LANES
    edge = capacity // LANES
    slab = slab_ref[0]
    nt = (((1,), (1,)), ((), ()))
    moments = jnp.concatenate([got_ref[:, c, :] for c in range(3)], axis=0)
    sum_re = lax.dot_general(moments, far_ref[0:8, :], nt, precision=HIGH, preferred_element_type=F32)
    sum_im = lax.dot_general(moments, far_ref[8:16, :], nt, precision=HIGH, preferred_element_type=F32)
    line = lax.broadcasted_iota(jnp.int32, (ROWS, MODES), 0)
    carry_re = jnp.zeros((ROWS, MODES), F32)
    carry_im = jnp.zeros((ROWS, MODES), F32)
    for index in range(3):
        weight = hop_ref[2 * index], hop_ref[2 * index + 1]
        for c in range(3):
            part = complex_mul(weight, (sum_re[c * slabs:(c + 1) * slabs], sum_im[c * slabs:(c + 1) * slabs]))
            part = complex_mul(part, (coef_ref[0], coef_ref[1]) if c < 2 else (coef_ref[2], coef_ref[3]))
            here = line == 8 * index + c
            carry_re = jnp.where(here, jnp.sum(part[0], axis=0, keepdims=True), carry_re)
            carry_im = jnp.where(here, jnp.sum(part[1], axis=0, keepdims=True), carry_im)
    plain = (((1,), (0,)), ((), ()))
    incoming = lax.dot_general(carry_re, near_ref[0:8, :], plain, precision=HIGH, preferred_element_type=F32) - lax.dot_general(
        carry_im, near_ref[8:16, :], plain, precision=HIGH, preferred_element_type=F32)
    ahead = jnp.maximum(slab - 1, 0) ^ FIRST_SLAB
    behind = jnp.minimum(slab + 1, slabs - 1) ^ FIRST_SLAB
    near_moments = jnp.concatenate([got_ref[ahead, 0:8, :], got_ref[slab ^ FIRST_SLAB, 0:8, :], got_ref[behind, 0:8, :]], axis=0)
    by_trans = lax.dot_general(near_moments, trans_ref[...], plain, precision=HIGH, preferred_element_type=F32)
    by_long = lax.dot_general(near_moments, long_ref[...], plain, precision=HIGH, preferred_element_type=F32)
    wide = lax.broadcasted_iota(jnp.int32, (ROWS, LANES), 0)
    kicks = jnp.where(wide % 8 == 2, by_long, by_trans) + incoming
    kick_ref[...] = kicks[8:11]

    for q in range(6):
        work_ref[q * ROWS:q * ROWS + edge, :] = got_ref[behind, edge * (q + 1):edge * (q + 2), :]
        work_ref[q * ROWS + edge:q * ROWS + edge + tiles, :] = dense_ref[q * tiles:(q + 1) * tiles, :]
        work_ref[q * ROWS + edge + tiles:q * ROWS + 2 * edge + tiles, :] = got_ref[ahead, edge * (q + 1):edge * (q + 2), :]
        work_ref[q * ROWS + 2 * edge + tiles:(q + 1) * ROWS, :] = jnp.zeros((ROWS - 2 * edge - tiles, LANES), F32)
    base = 6 * ROWS
    none = F32(-1.0)
    work_ref[base:base + edge, :] = jnp.where(slab < slabs - 1, got_ref[behind, 7 * edge:8 * edge, :], none)
    work_ref[base + edge:base + edge + tiles, :] = dense_ref[6 * tiles:7 * tiles, :]
    work_ref[base + edge + tiles:base + 2 * edge + tiles, :] = jnp.where(slab > 0, got_ref[ahead, 7 * edge:8 * edge, :], none)
    work_ref[base + 2 * edge + tiles:base + ROWS, :] = jnp.full((ROWS - 2 * edge - tiles, LANES), -1.0, F32)

    marks = work_ref[base:base + ROWS, :]
    kept = marks >= 0.0
    index = jnp.maximum(marks, 0.0).astype(jnp.int32)

    def kick_of(c):
        table = jnp.where(wide < edge, kicks[16 + c:17 + c], jnp.where(wide < edge + tiles, kicks[8 + c:9 + c], kicks[c:c + 1]))
        return jnp.take_along_axis(table, index, axis=1)

    x, px, y, py, s, e = [work_ref[q * ROWS:(q + 1) * ROWS, :] for q in range(6)]
    px = px + kick_of(0)
    py = py + kick_of(1)
    e = e + kick_of(2)
    jx = 0.5 * (x * x + px * px)
    jy = 0.5 * (y * y + py * py)
    ux = turn_reduce(0.269 + 0.05 * e + 0.02 * e * e + 0.03 * jx - 0.02 * jy)
    uy = turn_reduce(0.355 + 0.04 * e - 0.015 * e * e + 0.03 * jy - 0.02 * jx)
    cx, sx, cy, sy = cosine(ux), sine(ux), cosine(uy), sine(uy)
    e_new = e - 0.05 * (sine(radians_to_turns(0.3 + s)) - F32(math.sin(0.3)))
    s_new = s - 0.1 * e_new
    results = (cx * x + sx * px, cx * px - sx * x, cy * y + sy * py, cy * py - sy * y, s_new, e_new)
    for q, value in enumerate(results):
        done_ref[q * ROWS:(q + 1) * ROWS, :] = jnp.where(kept, value, F32(0.0))
    for tile in range(tiles + 2 * edge):
        out_ref[:, tile * LANES:(tile + 1) * LANES] = done_ref[pl.ds(tile, 6, stride=ROWS), :]


def specs(*kinds):
    return [pl.BlockSpec(memory_space={"s": pltpu.SMEM, "v": pltpu.VMEM, "h": pltpu.HBM}[kind]) for kind in kinds]


def stay(array):
    return pltpu.with_memory_space_constraint(array, pltpu.HBM)


def shape_of(*dims):
    return jax.ShapeDtypeStruct(dims, F32)


def body(particles, slice_index, moving, decay_rate, wake_freq, wake_amp):
    slabs = lax.axis_size("gz")
    members = lax.axis_size("pa")
    local = particles.shape[1]
    capacity = local * 3 // 16
    tiles = local // LANES
    fill = local * members / LANES
    slab = lax.axis_index("gz").astype(jnp.int32).reshape(1)
    index = slice_index.reshape(tiles, LANES)

    moments, dense, head, tail, near, far, trans, long, hop, coef = pl.pallas_call(
        functools.partial(deposit_kernel, slabs, local, capacity, fill),
        out_shape=[shape_of(members, 1, 3 * LANES), shape_of(7 * tiles, LANES), shape_of(ROWS, LANES), shape_of(ROWS, LANES),
                   shape_of(16, LANES), shape_of(16, LANES), shape_of(LANES, LANES), shape_of(LANES, LANES),
                   shape_of(6, slabs, MODES), shape_of(4, slabs, MODES)],
        in_specs=specs(*"shhhhhh"),
        out_specs=specs(*"vvvvvvvvvv"),
        scratch_shapes=[pltpu.VMEM((6, local), F32), pltpu.VMEM((tiles, LANES), jnp.int32), pltpu.SMEM((1, 1, 2), jnp.int32),
                        pltpu.SMEM((MODES,), F32), pltpu.SMEM((MODES,), F32), pltpu.SMEM((4, MODES), F32),
                        pltpu.SemaphoreType.DMA((6,))],
        compiler_params=SMALL,
        name="deposit",
    )(slab, *[stay(array) for array in (particles, index, moving, decay_rate, wake_freq, wake_amp)])

    chips = members // 2
    pairs = [[2 * z + 1, 2 * z] for z in range(chips)]
    rings = [[2 * ((z + FIRST_RING) % chips) + core for z in range(chips)] for core in range(2)]
    order = [slot ^ FIRST_SLAB for slot in range(slabs)]
    gathered = lax.all_to_all(moments, "pa", 0, 0, axis_index_groups=[[(2 * FIRST_RING + 1) ^ slot for slot in range(members)]])
    packed = pl.pallas_call(
        functools.partial(pack_kernel, slabs),
        out_shape=pltpu.VMEM((slabs, ROWS, LANES), F32),
        in_specs=specs(*"svvv"),
        out_specs=specs("v")[0],
        compiler_params=SMALL,
        name="pack",
    )(slab, gathered, head, tail)
    everyone = lax.all_to_all(packed, "gz", 0, 0, axis_index_groups=[order])
    return pl.pallas_call(
        functools.partial(finish_kernel, slabs, local, capacity),
        out_shape=[shape_of(3, LANES), shape_of(6, local + 2 * capacity)],
        in_specs=specs(*"svvvvvvvv"),
        out_specs=specs(*"vv"),
        scratch_shapes=[pltpu.VMEM((7 * ROWS, LANES), F32), pltpu.VMEM((6 * ROWS, LANES), F32)],
        compiler_params=SMALL,
        name="finish",
    )(slab, everyone, dense, near, far, trans, long, hop, coef)


def solution(mesh):
    return jax.shard_map(
        body,
        mesh=mesh,
        in_specs=(P(None, ("gz", "pa")), P(("gz", "pa")), P("gz", "pa", None), P(), P(), P()),
        out_specs=(P(None, "gz"), P(None, ("gz", "pa"))),
        check_vma=False,
    )
```

```python
import functools
import math

import jax
import jax.numpy as jnp
from jax import lax
from jax.experimental import pallas as pl
from jax.experimental.pallas import tpu as pltpu
from jax.sharding import PartitionSpec as P

LANES = 128
MODES = 8
ROWS = 24
HIGH = lax.Precision.HIGHEST
F32 = jnp.float32

COS_TERMS = (1.0, -19.73920440673828, 64.93911743164062, -85.45014190673828, 60.167633056640625,
             -25.967601776123047, 6.528658866882324)
SIN_TERMS = (6.2831854820251465, -41.34170150756836, 81.60513305664062, -76.70301818847656,
             42.02592849731445, -14.899847984313965, 3.238137722015381)
SMALL = pltpu.CompilerParams(vmem_limit_bytes=4 << 20)
FIRST_MEMBER = 17
CUTS = (8, 22)
FIRST_SLAB = 10
INV_TWO_PI = 0.15915494309189535
TURN_PARTS = (6.28125, 1.93500518798828125e-3, 3.0199159819567529e-7)


def horner(terms, t):
    total = jnp.full_like(t, terms[-1])
    for term in terms[-2::-1]:
        total = total * t + F32(term)
    return total


def turn_reduce(turns):
    return turns - jnp.floor(turns + F32(0.5))


def sine(turns):
    return turns * horner(SIN_TERMS, turns * turns)


def cosine(turns):
    return horner(COS_TERMS, turns * turns)


def radians_to_turns(angle):
    whole = jnp.floor(angle * F32(INV_TWO_PI) + F32(0.5))
    rest = angle
    for part in TURN_PARTS:
        rest = rest - whole * F32(part)
    return rest * F32(INV_TWO_PI)


def powers(damping, freq, distance):
    envelope = jnp.exp(-damping * distance)
    turns = radians_to_turns(freq * distance)
    return envelope * cosine(turns), envelope * sine(turns)


def complex_mul(a, b):
    return a[0] * b[0] - a[1] * b[1], a[0] * b[1] + a[1] * b[0]


def spread(read, shape, axis):
    where = lax.broadcasted_iota(jnp.int32, shape, axis) % MODES
    total = jnp.zeros(shape, F32)
    for mode in range(MODES):
        total = jnp.where(where == mode, read(mode), total)
    return total


def make_tables(slabs, width, slab_ref, decay_ref, freq_ref, amp_ref, near_ref, far_ref, trans_ref, long_ref, mix_ref):
    shape = (MODES, LANES)
    scale = F32(1.0 / (slabs * width))
    damping = spread(lambda m: decay_ref[m], shape, 0) * scale
    freq = spread(lambda m: freq_ref[m], shape, 0)
    amps = [spread(functools.partial(lambda row, m: amp_ref[row, m], row), shape, 0) for row in range(4)]
    distance = lax.broadcasted_iota(jnp.int32, shape, 1).astype(F32)
    near = powers(damping, freq, distance)
    far = powers(damping, freq, F32(width) - distance)
    near_ref[0:8, :] = near[0]
    near_ref[8:16, :] = -near[1]
    for block, half in enumerate((0, 1, 1, 0)):
        far_ref[8 * block:8 * block + 8, :] = far[half]
    norm_trans = jnp.sqrt(2.0 * damping)
    norm_long = jnp.sqrt(damping * damping + freq * freq)
    wave_trans = jnp.sum(norm_trans * (amps[0] * near[0] - amps[1] * near[1]), axis=0, keepdims=True)
    wave_long = jnp.sum(norm_long * (amps[2] * near[0] - amps[3] * near[1]), axis=0, keepdims=True)
    square = (LANES, LANES)
    later = lax.broadcasted_iota(jnp.int32, square, 1) > lax.broadcasted_iota(jnp.int32, square, 0)
    for wave, ref in ((wave_trans, trans_ref), (wave_long, long_ref)):
        shifted = pltpu.roll(jnp.broadcast_to(wave, square), 0, 1, stride=1, stride_axis=0)
        ref[...] = jnp.where(later, shifted, F32(0.0))

    small = (slabs, 2 * MODES)
    damping = spread(lambda m: decay_ref[m], small, 1) * scale
    freq = spread(lambda m: freq_ref[m], small, 1)
    amps = [spread(functools.partial(lambda row, m: amp_ref[row, m], row), small, 1) for row in range(4)]
    norm_trans = jnp.sqrt(2.0 * damping)
    norm_long = jnp.sqrt(damping * damping + freq * freq)
    coefs = (amps[0] * norm_trans, amps[1] * norm_trans), (amps[2] * norm_long, amps[3] * norm_long)
    sign = jnp.where(lax.broadcasted_iota(jnp.int32, small, 1) < MODES, F32(-1.0), F32(1.0))
    step = powers(damping, freq, jnp.full(small, width, F32))
    ladder = [step]
    while 2 ** len(ladder) < slabs:
        ladder.append(complex_mul(ladder[-1], ladder[-1]))
    source = lax.broadcasted_iota(jnp.int32, small, 0) ^ FIRST_SLAB
    for index in range(3):
        hops = slab_ref[0] + (index - 2) - source
        weight = (jnp.ones(small, F32), jnp.zeros(small, F32))
        for bit, factor in enumerate(ladder):
            longer = complex_mul(weight, factor)
            taken = (hops & (1 << bit)) != 0
            weight = tuple(jnp.where(taken, b, a) for a, b in zip(weight, longer))
        for kind, coef in enumerate(coefs):
            mixed = complex_mul(weight, coef)
            mix_ref[4 * index + 2 * kind] = jnp.where(hops >= 0, mixed[0], F32(0.0))
            mix_ref[4 * index + 2 * kind + 1] = jnp.where(hops >= 0, sign * mixed[1], F32(0.0))


def fetch(sources, targets, sems):
    copies = [pltpu.make_async_copy(a, b, sems.at[k]) for k, (a, b) in enumerate(zip(sources, targets))]
    for copy in copies:
        copy.start()
    for copy in copies:
        copy.wait()


def deposit(local, fill, part_ref, index_ref, moment_ref):
    tiles = local // LANES
    shape = (8, local)
    row = lax.broadcasted_iota(jnp.int32, shape, 0)
    base = jnp.where(row < 3, part_ref[0:1, :], jnp.where(row < 6, part_ref[2:3, :], F32(1.0)))
    bf = jnp.bfloat16
    high = base.astype(bf).astype(F32)
    rest = base - high
    mid = rest.astype(bf).astype(F32)
    low = rest - mid
    third = row % 3
    values = jnp.where(third == 0, high, jnp.where(third == 1, mid, low)).astype(bf)
    slot = lax.broadcasted_iota(jnp.int32, (LANES, LANES), 0)
    total = jnp.zeros((8, LANES), F32)
    group = 2
    for first in range(0, tiles, group):
        hot = jnp.concatenate(
            [(slot == index_ref[t:t + 1, :]).astype(F32).astype(bf) for t in range(first, first + group)], axis=1
        )
        total = total + lax.dot_general(
            values[:, first * LANES:(first + group) * LANES], hot, (((1,), (1,)), ((), ())), preferred_element_type=F32
        )
    root = F32(1.0 / math.sqrt(fill))
    sums = jnp.concatenate([
        (total[0:1] + total[1:2] + total[2:3]) * root,
        (total[3:4] + total[4:5] + total[5:6]) * root,
        total[6:7] * F32(1.0 / fill),
        jnp.zeros((1, LANES), F32),
    ], axis=0)
    for slot in range(moment_ref.shape[0]):
        for c in range(3):
            moment_ref[slot, :, c * LANES:(c + 1) * LANES] = sums[c:c + 1]


def make_payload(local, capacity, part_ref, index_ref, moving_ref, dense_ref, head_ref, tail_ref):
    tiles = local // LANES
    for tile in range(tiles):
        dense_ref[pl.ds(tile, 6, stride=tiles), :] = part_ref[:, tile * LANES:(tile + 1) * LANES]
    own = (tiles, LANES)
    position = lax.broadcasted_iota(jnp.int32, own, 0) * LANES + lax.broadcasted_iota(jnp.int32, own, 1)
    stays = (position >= moving_ref[0, 0, 0]) & (position < local - moving_ref[0, 0, 1])
    dense_ref[6 * tiles:7 * tiles, :] = jnp.where(stays, index_ref[...].astype(F32), F32(-1.0))
    edge = capacity // LANES
    place = lax.broadcasted_iota(jnp.int32, (edge, LANES), 0) * LANES + lax.broadcasted_iota(jnp.int32, (edge, LANES), 1)
    for ref, start, leaving in (
        (head_ref, 0, place < moving_ref[0, 0, 0]),
        (tail_ref, tiles - edge, place >= capacity - moving_ref[0, 0, 1]),
    ):
        ref[0:edge, :] = jnp.zeros((edge, LANES), F32)
        for q in range(6):
            ref[edge * (q + 1):edge * (q + 2), :] = dense_ref[q * tiles + start:q * tiles + start + edge, :]
        ref[edge * 7:edge * 8, :] = jnp.where(leaving, index_ref[start:start + edge, :].astype(F32), F32(-1.0))


def deposit_kernel(slabs, local, capacity, fill, slab_ref, part_hbm, index_hbm, moving_hbm, decay_hbm, freq_hbm, amp_hbm, *refs):
    outs, (part_ref, index_ref, moving_ref, decay_ref, freq_ref, amp_ref, sems) = refs[:9], refs[9:]
    fetch((part_hbm, index_hbm, moving_hbm, decay_hbm, freq_hbm, amp_hbm),
          (part_ref, index_ref, moving_ref, decay_ref, freq_ref, amp_ref), sems)
    deposit(local, fill, part_ref, index_ref, outs[0])
    make_payload(local, capacity, part_ref, index_ref, moving_ref, *outs[1:4])
    make_tables(slabs, LANES, slab_ref, decay_ref, freq_ref, amp_ref, *outs[4:])


def pack_kernel(slabs, slab_ref, got_ref, head_ref, tail_ref, out_ref):
    moments = got_ref[0]
    for source in range(1, got_ref.shape[0]):
        moments = moments + got_ref[source]
    head, tail = head_ref[...], tail_ref[...]
    for slot in range(slabs):
        out_ref[slot] = jnp.where((slot ^ FIRST_SLAB) < slab_ref[0], head, tail)
        for c in range(3):
            out_ref[slot, c:c + 1, :] = moments[:, c * LANES:(c + 1) * LANES]


def finish_kernel(slabs, local, capacity, slab_ref, got_ref, dense_ref, near_ref, far_ref, trans_ref, long_ref, mix_ref, kick_hbm, out_hbm, work_ref, done_ref, kick_ref, out_ref, sems):
    tiles = local // LANES
    edge = capacity // LANES
    slab = slab_ref[0]
    nt = (((1,), (1,)), ((), ()))
    moments = jnp.concatenate([got_ref[:, c, :] for c in range(3)], axis=0)
    sums = lax.dot_general(moments, far_ref[0:16, :], nt, precision=HIGH, preferred_element_type=F32)
    swapped = lax.dot_general(moments, far_ref[16:32, :], nt, precision=HIGH, preferred_element_type=F32)
    line = lax.broadcasted_iota(jnp.int32, (ROWS, 2 * MODES), 0)
    carry = jnp.zeros((ROWS, 2 * MODES), F32)
    for index in range(3):
        for c in range(3):
            mix = 4 * index + (2 if c == 2 else 0)
            rows = slice(c * slabs, (c + 1) * slabs)
            part = mix_ref[mix] * sums[rows] + mix_ref[mix + 1] * swapped[rows]
            carry = jnp.where(line == 8 * index + c, jnp.sum(part, axis=0, keepdims=True), carry)
    plain = (((1,), (0,)), ((), ()))
    incoming = lax.dot_general(carry, near_ref[...], plain, precision=HIGH, preferred_element_type=F32)
    ahead = jnp.maximum(slab - 1, 0) ^ FIRST_SLAB
    behind = jnp.minimum(slab + 1, slabs - 1) ^ FIRST_SLAB
    near_moments = jnp.concatenate([got_ref[ahead, 0:8, :], got_ref[slab ^ FIRST_SLAB, 0:8, :], got_ref[behind, 0:8, :]], axis=0)
    by_trans = lax.dot_general(near_moments, trans_ref[...], plain, precision=HIGH, preferred_element_type=F32)
    by_long = lax.dot_general(near_moments, long_ref[...], plain, precision=HIGH, preferred_element_type=F32)
    wide = lax.broadcasted_iota(jnp.int32, (ROWS, LANES), 0)
    kicks = jnp.where(wide % 8 == 2, by_long, by_trans) + incoming
    kick_ref[...] = kicks[8:11]
    copies = [pltpu.make_async_copy(kick_ref, kick_hbm, sems.at[0])]
    copies[0].start()

    for q in range(6):
        work_ref[q * ROWS:q * ROWS + edge, :] = got_ref[behind, edge * (q + 1):edge * (q + 2), :]
        work_ref[q * ROWS + edge:q * ROWS + edge + tiles, :] = dense_ref[q * tiles:(q + 1) * tiles, :]
        work_ref[q * ROWS + edge + tiles:q * ROWS + 2 * edge + tiles, :] = got_ref[ahead, edge * (q + 1):edge * (q + 2), :]
        work_ref[q * ROWS + 2 * edge + tiles:(q + 1) * ROWS, :] = jnp.zeros((ROWS - 2 * edge - tiles, LANES), F32)
    base = 6 * ROWS
    none = F32(-1.0)
    work_ref[base:base + edge, :] = jnp.where(slab < slabs - 1, got_ref[behind, 7 * edge:8 * edge, :], none)
    work_ref[base + edge:base + edge + tiles, :] = dense_ref[6 * tiles:7 * tiles, :]
    work_ref[base + edge + tiles:base + 2 * edge + tiles, :] = jnp.where(slab > 0, got_ref[ahead, 7 * edge:8 * edge, :], none)
    work_ref[base + 2 * edge + tiles:base + ROWS, :] = jnp.full((ROWS - 2 * edge - tiles, LANES), -1.0, F32)

    marks = work_ref[base:base + ROWS, :]
    kept = marks >= 0.0
    index = jnp.maximum(marks, 0.0).astype(jnp.int32)

    def kick_of(c):
        table = jnp.where(wide < edge, kicks[16 + c:17 + c], jnp.where(wide < edge + tiles, kicks[8 + c:9 + c], kicks[c:c + 1]))
        return jnp.take_along_axis(table, index, axis=1)

    x, px, y, py, s, e = [work_ref[q * ROWS:(q + 1) * ROWS, :] for q in range(6)]
    px = px + kick_of(0)
    py = py + kick_of(1)
    e = e + kick_of(2)
    jx = 0.5 * (x * x + px * px)
    jy = 0.5 * (y * y + py * py)
    ux = turn_reduce(0.269 + 0.05 * e + 0.02 * e * e + 0.03 * jx - 0.02 * jy)
    uy = turn_reduce(0.355 + 0.04 * e - 0.015 * e * e + 0.03 * jy - 0.02 * jx)
    cx, sx, cy, sy = cosine(ux), sine(ux), cosine(uy), sine(uy)
    e_new = e - 0.05 * (sine(radians_to_turns(0.3 + s)) - F32(math.sin(0.3)))
    s_new = s - 0.1 * e_new
    results = (cx * x + sx * px, cx * px - sx * x, cy * y + sy * py, cy * py - sy * y, s_new, e_new)
    for q, value in enumerate(results):
        done_ref[q * ROWS:(q + 1) * ROWS, :] = jnp.where(kept, value, F32(0.0))
    for tile in range(tiles + 2 * edge):
        out_ref[:, tile * LANES:(tile + 1) * LANES] = done_ref[pl.ds(tile, 6, stride=ROWS), :]
        if tile + 1 in CUTS:
            piece = slice(([0] + [cut for cut in CUTS if cut <= tile])[-1] * LANES, (tile + 1) * LANES)
            copies.append(pltpu.make_async_copy(out_ref.at[:, piece], out_hbm.at[:, piece], sems.at[len(copies)]))
            copies[-1].start()
    for copy in copies:
        copy.wait()


def specs(*kinds):
    return [pl.BlockSpec(memory_space={"s": pltpu.SMEM, "v": pltpu.VMEM, "h": pltpu.HBM}[kind]) for kind in kinds]


def stay(array):
    return pltpu.with_memory_space_constraint(array, pltpu.HBM)


def shape_of(*dims):
    return jax.ShapeDtypeStruct(dims, F32)


def body(particles, slice_index, moving, decay_rate, wake_freq, wake_amp):
    slabs = lax.axis_size("gz")
    members = lax.axis_size("pa")
    local = particles.shape[1]
    capacity = local * 3 // 16
    tiles = local // LANES
    fill = local * members / LANES
    slab = lax.axis_index("gz").astype(jnp.int32).reshape(1)
    index = slice_index.reshape(tiles, LANES)

    moments, dense, head, tail, near, far, trans, long, mix = pl.pallas_call(
        functools.partial(deposit_kernel, slabs, local, capacity, fill),
        out_shape=[shape_of(members, 1, 3 * LANES), shape_of(7 * tiles, LANES), shape_of(ROWS, LANES), shape_of(ROWS, LANES),
                   shape_of(16, LANES), shape_of(32, LANES), shape_of(LANES, LANES), shape_of(LANES, LANES),
                   shape_of(12, slabs, 2 * MODES)],
        in_specs=specs(*"shhhhhh"),
        out_specs=specs(*"vvvvvvvvv"),
        scratch_shapes=[pltpu.VMEM((6, local), F32), pltpu.VMEM((tiles, LANES), jnp.int32), pltpu.SMEM((1, 1, 2), jnp.int32),
                        pltpu.SMEM((MODES,), F32), pltpu.SMEM((MODES,), F32), pltpu.SMEM((4, MODES), F32),
                        pltpu.SemaphoreType.DMA((6,))],
        compiler_params=SMALL,
        name="deposit",
    )(slab, *[stay(array) for array in (particles, index, moving, decay_rate, wake_freq, wake_amp)])

    order = [slot ^ FIRST_SLAB for slot in range(slabs)]
    gathered = lax.all_to_all(moments, "pa", 0, 0, axis_index_groups=[[FIRST_MEMBER ^ slot for slot in range(members)]])
    packed = pl.pallas_call(
        functools.partial(pack_kernel, slabs),
        out_shape=shape_of(slabs, ROWS, LANES),
        in_specs=specs(*"svvv"),
        out_specs=specs("v")[0],
        compiler_params=SMALL,
        name="pack",
    )(slab, gathered, head, tail)
    everyone = lax.all_to_all(packed, "gz", 0, 0, axis_index_groups=[order])
    return pl.pallas_call(
        functools.partial(finish_kernel, slabs, local, capacity),
        out_shape=[shape_of(3, LANES), shape_of(6, local + 2 * capacity)],
        in_specs=specs(*"svvvvvvv"),
        out_specs=specs(*"hh"),
        scratch_shapes=[pltpu.VMEM((7 * ROWS, LANES), F32), pltpu.VMEM((6 * ROWS, LANES), F32), pltpu.VMEM((3, LANES), F32),
                        pltpu.VMEM((6, local + 2 * capacity), F32), pltpu.SemaphoreType.DMA((1 + len(CUTS),))],
        compiler_params=SMALL,
        name="finish",
    )(slab, everyone, dense, near, far, trans, long, mix)


def solution(mesh):
    return jax.shard_map(
        body,
        mesh=mesh,
        in_specs=(P(None, ("gz", "pa")), P(("gz", "pa")), P("gz", "pa", None), P(), P(), P()),
        out_specs=(P(None, "gz"), P(None, ("gz", "pa"))),
        check_vma=False,
    )
```

```python
import functools
import math

import jax
import jax.numpy as jnp
from jax import lax
from jax.experimental import pallas as pl
from jax.experimental.pallas import tpu as pltpu
from jax.sharding import PartitionSpec as P

LANES = 128
MODES = 8
ROWS = 24
HIGH = lax.Precision.HIGHEST
F32 = jnp.float32

COS_TERMS = (1.0, -19.73920440673828, 64.93911743164062, -85.45014190673828, 60.167633056640625,
             -25.967601776123047, 6.528658866882324)
SIN_TERMS = (6.2831854820251465, -41.34170150756836, 81.60513305664062, -76.70301818847656,
             42.02592849731445, -14.899847984313965, 3.238137722015381)
SMALL = pltpu.CompilerParams(vmem_limit_bytes=4 << 20)
FIRST_MEMBER = 17
CUTS = (8, 22)
FIRST_SLAB = 10
INV_TWO_PI = 0.15915494309189535
TURN_PARTS = (6.28125, 1.93500518798828125e-3, 3.0199159819567529e-7)


def horner(terms, t):
    total = jnp.full_like(t, terms[-1])
    for term in terms[-2::-1]:
        total = total * t + F32(term)
    return total


def turn_reduce(turns):
    return turns - jnp.floor(turns + F32(0.5))


def sine(turns):
    return turns * horner(SIN_TERMS, turns * turns)


def cosine(turns):
    return horner(COS_TERMS, turns * turns)


def radians_to_turns(angle):
    whole = jnp.floor(angle * F32(INV_TWO_PI) + F32(0.5))
    rest = angle
    for part in TURN_PARTS:
        rest = rest - whole * F32(part)
    return rest * F32(INV_TWO_PI)


def powers(damping, freq, distance):
    envelope = jnp.exp(-damping * distance)
    turns = radians_to_turns(freq * distance)
    return envelope * cosine(turns), envelope * sine(turns)


def complex_mul(a, b):
    return a[0] * b[0] - a[1] * b[1], a[0] * b[1] + a[1] * b[0]


def spread(read, shape, axis):
    where = lax.broadcasted_iota(jnp.int32, shape, axis) % MODES
    total = jnp.zeros(shape, F32)
    for mode in range(MODES):
        total = jnp.where(where == mode, read(mode), total)
    return total


def make_tables(slabs, width, slab_ref, decay_ref, freq_ref, amp_ref, near_ref, far_ref, local_ref, mix_ref):
    shape = (MODES, LANES)
    scale = F32(1.0 / (slabs * width))
    damping = spread(lambda m: decay_ref[m], shape, 0) * scale
    freq = spread(lambda m: freq_ref[m], shape, 0)
    amps = [spread(functools.partial(lambda row, m: amp_ref[row, m], row), shape, 0) for row in range(4)]
    distance = lax.broadcasted_iota(jnp.int32, shape, 1).astype(F32)
    near = powers(damping, freq, distance)
    far = powers(damping, freq, F32(width) - distance)
    for block, half in enumerate((0, 1, 1, 0)):
        far_ref[8 * block:8 * block + 8, :] = far[half]
        near_ref[8 * block:8 * block + 8, :] = near[0] if block % 2 == 0 else -near[1]
    norm_trans = jnp.sqrt(2.0 * damping)
    norm_long = jnp.sqrt(damping * damping + freq * freq)
    wave_trans = jnp.sum(norm_trans * (amps[0] * near[0] - amps[1] * near[1]), axis=0, keepdims=True)
    wave_long = jnp.sum(norm_long * (amps[2] * near[0] - amps[3] * near[1]), axis=0, keepdims=True)
    square = (LANES, LANES)
    later = lax.broadcasted_iota(jnp.int32, square, 1) > lax.broadcasted_iota(jnp.int32, square, 0)
    for kind, wave in enumerate((wave_trans, wave_long)):
        shifted = pltpu.roll(jnp.broadcast_to(wave, square), 0, 1, stride=1, stride_axis=0)
        local_ref[:, kind * LANES:(kind + 1) * LANES] = jnp.where(later, shifted, F32(0.0))

    small = (slabs, 4 * MODES)
    damping = spread(lambda m: decay_ref[m], small, 1) * scale
    freq = spread(lambda m: freq_ref[m], small, 1)
    amps = [spread(functools.partial(lambda row, m: amp_ref[row, m], row), small, 1) for row in range(4)]
    norm_trans = jnp.sqrt(2.0 * damping)
    norm_long = jnp.sqrt(damping * damping + freq * freq)
    coefs = (amps[0] * norm_trans, amps[1] * norm_trans), (amps[2] * norm_long, amps[3] * norm_long)
    lane = lax.broadcasted_iota(jnp.int32, small, 1)
    sign = jnp.where(lane < 3 * MODES, F32(-1.0), F32(1.0))
    step = powers(damping, freq, jnp.full(small, width, F32))
    ladder = [step]
    while 2 ** len(ladder) < slabs:
        ladder.append(complex_mul(ladder[-1], ladder[-1]))
    source = slab_of(lax.broadcasted_iota(jnp.int32, small, 0), slabs)
    for index in range(3):
        hops = slab_ref[0] + (index - 2) - source
        weight = (jnp.ones(small, F32), jnp.zeros(small, F32))
        for bit, factor in enumerate(ladder):
            longer = complex_mul(weight, factor)
            taken = (hops & (1 << bit)) != 0
            weight = tuple(jnp.where(taken, b, a) for a, b in zip(weight, longer))
        for kind, coef in enumerate(coefs):
            mixed = complex_mul(weight, coef)
            both = jnp.where(lane < 2 * MODES, mixed[0], sign * mixed[1])
            mix_ref[2 * index + kind] = jnp.where(hops >= 0, both, F32(0.0))


def slab_of(slot, slabs):
    return (slot + FIRST_SLAB) % slabs


def slot_of(slab, slabs):
    return (slab + slabs - FIRST_SLAB) % slabs


def fetch(sources, targets, sems):
    copies = [pltpu.make_async_copy(a, b, sems.at[k]) for k, (a, b) in enumerate(zip(sources, targets))]
    for copy in copies:
        copy.start()
    for copy in copies:
        copy.wait()


def deposit(local, fill, part_ref, index_ref, moment_ref):
    tiles = local // LANES
    shape = (8, local)
    row = lax.broadcasted_iota(jnp.int32, shape, 0)
    base = jnp.where(row < 3, part_ref[0:1, :], jnp.where(row < 6, part_ref[2:3, :], F32(1.0)))
    bf = jnp.bfloat16
    high = base.astype(bf).astype(F32)
    rest = base - high
    mid = rest.astype(bf).astype(F32)
    low = rest - mid
    third = row % 3
    values = jnp.where(third == 0, high, jnp.where(third == 1, mid, low)).astype(bf)
    slot = lax.broadcasted_iota(jnp.int32, (LANES, LANES), 0)
    total = jnp.zeros((8, LANES), F32)
    group = 2
    for first in range(0, tiles, group):
        hot = jnp.concatenate(
            [(slot == index_ref[t:t + 1, :]).astype(F32).astype(bf) for t in range(first, first + group)], axis=1
        )
        total = total + lax.dot_general(
            values[:, first * LANES:(first + group) * LANES], hot, (((1,), (1,)), ((), ())), preferred_element_type=F32
        )
    root = F32(1.0 / math.sqrt(fill))
    sums = (
        (total[0:1] + total[1:2] + total[2:3]) * root,
        (total[3:4] + total[4:5] + total[5:6]) * root,
        total[6:7] * F32(1.0 / fill),
    )
    third = lax.broadcasted_iota(jnp.int32, (ROWS, LANES), 0) % 3
    block = jnp.where(third == 0, sums[0], jnp.where(third == 1, sums[1], sums[2]))
    for start in range(0, moment_ref.shape[0], ROWS):
        moment_ref[start:start + ROWS, :] = block


def make_payload(local, capacity, part_ref, index_ref, moving_ref, dense_ref, head_ref, tail_ref):
    tiles = local // LANES
    for tile in range(tiles):
        dense_ref[pl.ds(tile, 6, stride=tiles), :] = part_ref[:, tile * LANES:(tile + 1) * LANES]
    own = (tiles, LANES)
    position = lax.broadcasted_iota(jnp.int32, own, 0) * LANES + lax.broadcasted_iota(jnp.int32, own, 1)
    stays = (position >= moving_ref[0, 0, 0]) & (position < local - moving_ref[0, 0, 1])
    dense_ref[6 * tiles:7 * tiles, :] = jnp.where(stays, index_ref[...].astype(F32), F32(-1.0))
    edge = capacity // LANES
    place = lax.broadcasted_iota(jnp.int32, (edge, LANES), 0) * LANES + lax.broadcasted_iota(jnp.int32, (edge, LANES), 1)
    for ref, start, leaving in (
        (head_ref, 0, place < moving_ref[0, 0, 0]),
        (tail_ref, tiles - edge, place >= capacity - moving_ref[0, 0, 1]),
    ):
        ref[0:edge, :] = jnp.zeros((edge, LANES), F32)
        for q in range(6):
            ref[edge * (q + 1):edge * (q + 2), :] = dense_ref[q * tiles + start:q * tiles + start + edge, :]
        ref[edge * 7:edge * 8, :] = jnp.where(leaving, index_ref[start:start + edge, :].astype(F32), F32(-1.0))


def deposit_kernel(slabs, local, capacity, fill, slab_ref, part_hbm, index_hbm, moving_hbm, decay_hbm, freq_hbm, amp_hbm, *refs):
    outs, (part_ref, index_ref, moving_ref, decay_ref, freq_ref, amp_ref, sems) = refs[:8], refs[8:]
    fetch((part_hbm, index_hbm, moving_hbm, decay_hbm, freq_hbm, amp_hbm),
          (part_ref, index_ref, moving_ref, decay_ref, freq_ref, amp_ref), sems)
    deposit(local, fill, part_ref, index_ref, outs[0])
    make_payload(local, capacity, part_ref, index_ref, moving_ref, *outs[1:4])
    make_tables(slabs, LANES, slab_ref, decay_ref, freq_ref, amp_ref, *outs[4:])


def pack_kernel(slabs, slab_ref, got_ref, head_ref, tail_ref, out_ref):
    moments = got_ref[0]
    for source in range(1, got_ref.shape[0]):
        moments = moments + got_ref[source]
    head, tail = head_ref[...], tail_ref[...]
    for slot in range(slabs):
        out_ref[slot] = jnp.where(slab_of(slot, slabs) < slab_ref[0], head, tail)
        for c in range(3):
            out_ref[slot, c:c + 1, :] = moments[:, c * LANES:(c + 1) * LANES]


def finish_kernel(slabs, local, capacity, slab_ref, got_ref, dense_ref, near_ref, far_ref, local_ref, mix_ref, kick_hbm, out_hbm, work_ref, done_ref, kick_ref, out_ref, sems):
    tiles = local // LANES
    edge = capacity // LANES
    slab = slab_ref[0]
    nt = (((1,), (1,)), ((), ()))
    moments = jnp.concatenate([got_ref[:, c, :] for c in range(3)], axis=0)
    sums = lax.dot_general(moments, far_ref[...], nt, precision=HIGH, preferred_element_type=F32)
    line = lax.broadcasted_iota(jnp.int32, (ROWS, 4 * MODES), 0)
    carry = jnp.zeros((ROWS, 4 * MODES), F32)
    for index in range(3):
        for c in range(3):
            part = mix_ref[2 * index + (c == 2)] * sums[c * slabs:(c + 1) * slabs]
            carry = jnp.where(line == 8 * index + c, jnp.sum(part, axis=0, keepdims=True), carry)
    plain = (((1,), (0,)), ((), ()))
    incoming = lax.dot_general(carry, near_ref[...], plain, precision=HIGH, preferred_element_type=F32)
    ahead = slot_of(jnp.maximum(slab - 1, 0), slabs)
    behind = slot_of(jnp.minimum(slab + 1, slabs - 1), slabs)
    near_moments = jnp.concatenate([got_ref[ahead, 0:8, :], got_ref[slot_of(slab, slabs), 0:8, :], got_ref[behind, 0:8, :]], axis=0)
    local_kick = lax.dot_general(near_moments, local_ref[...], plain, precision=HIGH, preferred_element_type=F32)
    wide = lax.broadcasted_iota(jnp.int32, (ROWS, LANES), 0)
    kicks = jnp.where(wide % 8 == 2, local_kick[:, LANES:], local_kick[:, :LANES]) + incoming
    kick_ref[...] = kicks[8:11]
    copies = [pltpu.make_async_copy(kick_ref, kick_hbm, sems.at[0])]
    copies[0].start()

    for q in range(6):
        work_ref[q * ROWS:q * ROWS + edge, :] = got_ref[behind, edge * (q + 1):edge * (q + 2), :]
        work_ref[q * ROWS + edge:q * ROWS + edge + tiles, :] = dense_ref[q * tiles:(q + 1) * tiles, :]
        work_ref[q * ROWS + edge + tiles:q * ROWS + 2 * edge + tiles, :] = got_ref[ahead, edge * (q + 1):edge * (q + 2), :]
        work_ref[q * ROWS + 2 * edge + tiles:(q + 1) * ROWS, :] = jnp.zeros((ROWS - 2 * edge - tiles, LANES), F32)
    base = 6 * ROWS
    none = F32(-1.0)
    work_ref[base:base + edge, :] = jnp.where(slab < slabs - 1, got_ref[behind, 7 * edge:8 * edge, :], none)
    work_ref[base + edge:base + edge + tiles, :] = dense_ref[6 * tiles:7 * tiles, :]
    work_ref[base + edge + tiles:base + 2 * edge + tiles, :] = jnp.where(slab > 0, got_ref[ahead, 7 * edge:8 * edge, :], none)
    work_ref[base + 2 * edge + tiles:base + ROWS, :] = jnp.full((ROWS - 2 * edge - tiles, LANES), -1.0, F32)

    marks = work_ref[base:base + ROWS, :]
    kept = marks >= 0.0
    index = jnp.maximum(marks, 0.0).astype(jnp.int32)

    def kick_of(c):
        table = jnp.where(wide < edge, kicks[16 + c:17 + c], jnp.where(wide < edge + tiles, kicks[8 + c:9 + c], kicks[c:c + 1]))
        return jnp.take_along_axis(table, index, axis=1)

    x, px, y, py, s, e = [work_ref[q * ROWS:(q + 1) * ROWS, :] for q in range(6)]
    px = px + kick_of(0)
    py = py + kick_of(1)
    e = e + kick_of(2)
    jx = 0.5 * (x * x + px * px)
    jy = 0.5 * (y * y + py * py)
    ux = turn_reduce(0.269 + 0.05 * e + 0.02 * e * e + 0.03 * jx - 0.02 * jy)
    uy = turn_reduce(0.355 + 0.04 * e - 0.015 * e * e + 0.03 * jy - 0.02 * jx)
    cx, sx, cy, sy = cosine(ux), sine(ux), cosine(uy), sine(uy)
    e_new = e - 0.05 * (sine(radians_to_turns(0.3 + s)) - F32(math.sin(0.3)))
    s_new = s - 0.1 * e_new
    results = (cx * x + sx * px, cx * px - sx * x, cy * y + sy * py, cy * py - sy * y, s_new, e_new)
    for q, value in enumerate(results):
        done_ref[q * ROWS:(q + 1) * ROWS, :] = jnp.where(kept, value, F32(0.0))
    for tile in range(tiles + 2 * edge):
        out_ref[:, tile * LANES:(tile + 1) * LANES] = done_ref[pl.ds(tile, 6, stride=ROWS), :]
        if tile + 1 in CUTS:
            piece = slice(([0] + [cut for cut in CUTS if cut <= tile])[-1] * LANES, (tile + 1) * LANES)
            copies.append(pltpu.make_async_copy(out_ref.at[:, piece], out_hbm.at[:, piece], sems.at[len(copies)]))
            copies[-1].start()
    for copy in copies:
        copy.wait()


def specs(*kinds):
    return [pl.BlockSpec(memory_space={"s": pltpu.SMEM, "v": pltpu.VMEM, "h": pltpu.HBM}[kind]) for kind in kinds]


def stay(array):
    return pltpu.with_memory_space_constraint(array, pltpu.HBM)


def shape_of(*dims):
    return jax.ShapeDtypeStruct(dims, F32)


def body(particles, slice_index, moving, decay_rate, wake_freq, wake_amp):
    slabs = lax.axis_size("gz")
    members = lax.axis_size("pa")
    local = particles.shape[1]
    capacity = local * 3 // 16
    tiles = local // LANES
    fill = local * members / LANES
    slab = lax.axis_index("gz").astype(jnp.int32).reshape(1)
    index = slice_index.reshape(tiles, LANES)

    moments, dense, head, tail, near, far, toeplitz, mix = pl.pallas_call(
        functools.partial(deposit_kernel, slabs, local, capacity, fill),
        out_shape=[shape_of(3 * members, LANES), shape_of(7 * tiles, LANES), shape_of(ROWS, LANES), shape_of(ROWS, LANES),
                   shape_of(32, LANES), shape_of(32, LANES), shape_of(LANES, 2 * LANES), shape_of(6, slabs, 4 * MODES)],
        in_specs=specs(*"shhhhhh"),
        out_specs=specs(*"vvvvvvvv"),
        scratch_shapes=[pltpu.VMEM((6, local), F32), pltpu.VMEM((tiles, LANES), jnp.int32), pltpu.SMEM((1, 1, 2), jnp.int32),
                        pltpu.SMEM((MODES,), F32), pltpu.SMEM((MODES,), F32), pltpu.SMEM((4, MODES), F32),
                        pltpu.SemaphoreType.DMA((6,))],
        compiler_params=SMALL,
        name="deposit",
    )(slab, *[stay(array) for array in (particles, index, moving, decay_rate, wake_freq, wake_amp)])

    order = [slab_of(slot, slabs) for slot in range(slabs)]
    gathered = lax.all_to_all(moments.reshape(members, 1, 3 * LANES), "pa", 0, 0, axis_index_groups=[[FIRST_MEMBER ^ slot for slot in range(members)]])
    packed = pl.pallas_call(
        functools.partial(pack_kernel, slabs),
        out_shape=shape_of(slabs, ROWS, LANES),
        in_specs=specs(*"svvv"),
        out_specs=specs("v")[0],
        compiler_params=SMALL,
        name="pack",
    )(slab, gathered, head, tail)
    everyone = lax.all_to_all(packed, "gz", 0, 0, axis_index_groups=[order])
    return pl.pallas_call(
        functools.partial(finish_kernel, slabs, local, capacity),
        out_shape=[shape_of(3, LANES), shape_of(6, local + 2 * capacity)],
        in_specs=specs(*"svvvvvv"),
        out_specs=specs(*"hh"),
        scratch_shapes=[pltpu.VMEM((7 * ROWS, LANES), F32), pltpu.VMEM((6 * ROWS, LANES), F32), pltpu.VMEM((3, LANES), F32),
                        pltpu.VMEM((6, local + 2 * capacity), F32), pltpu.SemaphoreType.DMA((1 + len(CUTS),))],
        compiler_params=SMALL,
        name="finish",
    )(slab, everyone, dense, near, far, toeplitz, mix)


def solution(mesh):
    return jax.shard_map(
        body,
        mesh=mesh,
        in_specs=(P(None, ("gz", "pa")), P(("gz", "pa")), P("gz", "pa", None), P(), P(), P()),
        out_specs=(P(None, "gz"), P(None, ("gz", "pa"))),
        check_vma=False,
    )
```

```python
import functools
import math

import jax
import jax.numpy as jnp
from jax import lax
from jax.experimental import pallas as pl
from jax.experimental.pallas import tpu as pltpu
from jax.sharding import PartitionSpec as P

LANES = 128
MODES = 8
ROWS = 24
HIGH = lax.Precision.HIGHEST
F32 = jnp.float32

COS_TERMS = (1.0, -19.73920440673828, 64.93911743164062, -85.45014190673828, 60.167633056640625,
             -25.967601776123047, 6.528658866882324)
SIN_TERMS = (6.2831854820251465, -41.34170150756836, 81.60513305664062, -76.70301818847656,
             42.02592849731445, -14.899847984313965, 3.238137722015381)
SMALL = pltpu.CompilerParams(vmem_limit_bytes=4 << 20)
FIRST_MEMBER = 17
CUTS = (8, 22)
FIRST_SLAB = 10
INV_TWO_PI = 0.15915494309189535
TURN_PARTS = (6.28125, 1.93500518798828125e-3, 3.0199159819567529e-7)


def horner(terms, t):
    total = jnp.full_like(t, terms[-1])
    for term in terms[-2::-1]:
        total = total * t + F32(term)
    return total


def turn_reduce(turns):
    return turns - jnp.floor(turns + F32(0.5))


def sine(turns):
    return turns * horner(SIN_TERMS, turns * turns)


def cosine(turns):
    return horner(COS_TERMS, turns * turns)


def radians_to_turns(angle):
    whole = jnp.floor(angle * F32(INV_TWO_PI) + F32(0.5))
    rest = angle
    for part in TURN_PARTS:
        rest = rest - whole * F32(part)
    return rest * F32(INV_TWO_PI)


def powers(damping, freq, distance):
    envelope = jnp.exp(-damping * distance)
    turns = radians_to_turns(freq * distance)
    return envelope * cosine(turns), envelope * sine(turns)


def complex_mul(a, b):
    return a[0] * b[0] - a[1] * b[1], a[0] * b[1] + a[1] * b[0]


def spread(read, shape, axis):
    where = lax.broadcasted_iota(jnp.int32, shape, axis) % MODES
    total = jnp.zeros(shape, F32)
    for mode in range(MODES):
        total = jnp.where(where == mode, read(mode), total)
    return total


def make_tables(slabs, width, slab_ref, decay_ref, freq_ref, amp_ref, near_ref, far_ref, local_ref, mix_ref):
    shape = (MODES, LANES)
    scale = F32(1.0 / (slabs * width))
    damping = spread(lambda m: decay_ref[m], shape, 0) * scale
    freq = spread(lambda m: freq_ref[m], shape, 0)
    amps = [spread(functools.partial(lambda row, m: amp_ref[row, m], row), shape, 0) for row in range(4)]
    distance = lax.broadcasted_iota(jnp.int32, shape, 1).astype(F32)
    near = powers(damping, freq, distance)
    far = powers(damping, freq, F32(width) - distance)
    for block, half in enumerate((0, 1, 1, 0)):
        far_ref[8 * block:8 * block + 8, :] = far[half]
        near_ref[8 * block:8 * block + 8, :] = near[0] if block % 2 == 0 else -near[1]
    norm_trans = jnp.sqrt(2.0 * damping)
    norm_long = jnp.sqrt(damping * damping + freq * freq)
    wave_trans = jnp.sum(norm_trans * (amps[0] * near[0] - amps[1] * near[1]), axis=0, keepdims=True)
    wave_long = jnp.sum(norm_long * (amps[2] * near[0] - amps[3] * near[1]), axis=0, keepdims=True)
    square = (LANES, LANES)
    later = lax.broadcasted_iota(jnp.int32, square, 1) > lax.broadcasted_iota(jnp.int32, square, 0)
    for kind, wave in enumerate((wave_trans, wave_long)):
        shifted = pltpu.roll(jnp.broadcast_to(wave, square), 0, 1, stride=1, stride_axis=0)
        local_ref[:, kind * LANES:(kind + 1) * LANES] = jnp.where(later, shifted, F32(0.0))

    small = (slabs, 4 * MODES)
    damping = spread(lambda m: decay_ref[m], small, 1) * scale
    freq = spread(lambda m: freq_ref[m], small, 1)
    amps = [spread(functools.partial(lambda row, m: amp_ref[row, m], row), small, 1) for row in range(4)]
    norm_trans = jnp.sqrt(2.0 * damping)
    norm_long = jnp.sqrt(damping * damping + freq * freq)
    coefs = (amps[0] * norm_trans, amps[1] * norm_trans), (amps[2] * norm_long, amps[3] * norm_long)
    lane = lax.broadcasted_iota(jnp.int32, small, 1)
    sign = jnp.where(lane < 3 * MODES, F32(-1.0), F32(1.0))
    step = powers(damping, freq, jnp.full(small, width, F32))
    ladder = [step]
    while 2 ** len(ladder) < slabs:
        ladder.append(complex_mul(ladder[-1], ladder[-1]))
    source = slab_of(lax.broadcasted_iota(jnp.int32, small, 0), slabs)
    for index in range(3):
        hops = slab_ref[0] + (index - 2) - source
        weight = (jnp.ones(small, F32), jnp.zeros(small, F32))
        for bit, factor in enumerate(ladder):
            longer = complex_mul(weight, factor)
            taken = (hops & (1 << bit)) != 0
            weight = tuple(jnp.where(taken, b, a) for a, b in zip(weight, longer))
        for kind, coef in enumerate(coefs):
            mixed = complex_mul(weight, coef)
            both = jnp.where(lane < 2 * MODES, mixed[0], sign * mixed[1])
            mix_ref[2 * index + kind] = jnp.where(hops >= 0, both, F32(0.0))


def slab_of(slot, slabs):
    return (slot + FIRST_SLAB) % slabs


def slot_of(slab, slabs):
    return (slab + slabs - FIRST_SLAB) % slabs


def fetch(sources, targets, sems):
    copies = [pltpu.make_async_copy(a, b, sems.at[k]) for k, (a, b) in enumerate(zip(sources, targets))]
    for copy in copies:
        copy.start()
    for copy in copies:
        copy.wait()


def deposit(local, fill, part_ref, index_ref, moment_ref):
    tiles = local // LANES
    shape = (8, local)
    row = lax.broadcasted_iota(jnp.int32, shape, 0)
    base = jnp.where(row < 3, part_ref[0:1, :], jnp.where(row < 6, part_ref[2:3, :], F32(1.0)))
    bf = jnp.bfloat16
    high = base.astype(bf).astype(F32)
    rest = base - high
    mid = rest.astype(bf).astype(F32)
    low = rest - mid
    third = row % 3
    values = jnp.where(third == 0, high, jnp.where(third == 1, mid, low)).astype(bf)
    slot = lax.broadcasted_iota(jnp.int32, (LANES, LANES), 0)
    total = jnp.zeros((8, LANES), F32)
    group = 2
    for first in range(0, tiles, group):
        hot = jnp.concatenate(
            [(slot == index_ref[t:t + 1, :]).astype(F32).astype(bf) for t in range(first, first + group)], axis=1
        )
        total = total + lax.dot_general(
            values[:, first * LANES:(first + group) * LANES], hot, (((1,), (1,)), ((), ())), preferred_element_type=F32
        )
    root = F32(1.0 / math.sqrt(fill))
    sums = (
        (total[0:1] + total[1:2] + total[2:3]) * root,
        (total[3:4] + total[4:5] + total[5:6]) * root,
        total[6:7] * F32(1.0 / fill),
    )
    third = lax.broadcasted_iota(jnp.int32, (ROWS, LANES), 0) % 3
    block = jnp.where(third == 0, sums[0], jnp.where(third == 1, sums[1], sums[2]))
    for start in range(0, moment_ref.shape[0], ROWS):
        moment_ref[start:start + ROWS, :] = block


def make_payload(local, capacity, part_ref, index_ref, moving_ref, dense_ref, head_ref, tail_ref):
    tiles = local // LANES
    for tile in range(tiles):
        dense_ref[pl.ds(tile, 6, stride=tiles), :] = part_ref[:, tile * LANES:(tile + 1) * LANES]
    own = (tiles, LANES)
    position = lax.broadcasted_iota(jnp.int32, own, 0) * LANES + lax.broadcasted_iota(jnp.int32, own, 1)
    stays = (position >= moving_ref[0, 0, 0]) & (position < local - moving_ref[0, 0, 1])
    dense_ref[6 * tiles:7 * tiles, :] = jnp.where(stays, index_ref[...].astype(F32), F32(-1.0))
    edge = capacity // LANES
    place = lax.broadcasted_iota(jnp.int32, (edge, LANES), 0) * LANES + lax.broadcasted_iota(jnp.int32, (edge, LANES), 1)
    for ref, start, leaving in (
        (head_ref, 0, place < moving_ref[0, 0, 0]),
        (tail_ref, tiles - edge, place >= capacity - moving_ref[0, 0, 1]),
    ):
        ref[0:edge, :] = jnp.zeros((edge, LANES), F32)
        for q in range(6):
            ref[edge * (q + 1):edge * (q + 2), :] = dense_ref[q * tiles + start:q * tiles + start + edge, :]
        ref[edge * 7:edge * 8, :] = jnp.where(leaving, index_ref[start:start + edge, :].astype(F32), F32(-1.0))


def deposit_kernel(slabs, local, capacity, fill, slab_ref, part_hbm, index_hbm, moving_hbm, decay_hbm, freq_hbm, amp_hbm, *refs):
    outs, (part_ref, index_ref, moving_ref, decay_ref, freq_ref, amp_ref, sems) = refs[:8], refs[8:]
    fetch((part_hbm, index_hbm, moving_hbm, decay_hbm, freq_hbm, amp_hbm),
          (part_ref, index_ref, moving_ref, decay_ref, freq_ref, amp_ref), sems)
    deposit(local, fill, part_ref, index_ref, outs[0])
    make_payload(local, capacity, part_ref, index_ref, moving_ref, *outs[1:4])
    make_tables(slabs, LANES, slab_ref, decay_ref, freq_ref, amp_ref, *outs[4:])


def pack_kernel(slabs, slab_ref, got_ref, head_ref, tail_ref, out_ref):
    moments = got_ref[0]
    for source in range(1, got_ref.shape[0]):
        moments = moments + got_ref[source]
    head, tail = head_ref[...], tail_ref[...]
    for slot in range(slabs):
        out_ref[slot] = jnp.where(slab_of(slot, slabs) < slab_ref[0], head, tail)
        for c in range(3):
            out_ref[slot, c:c + 1, :] = moments[:, c * LANES:(c + 1) * LANES]


def finish_kernel(slabs, local, capacity, slab_ref, got_ref, dense_ref, near_ref, far_ref, local_ref, mix_ref, kick_hbm, out_hbm, work_ref, done_ref, kick_ref, out_ref, sems):
    tiles = local // LANES
    edge = capacity // LANES
    slab = slab_ref[0]
    nt = (((1,), (1,)), ((), ()))
    moments = jnp.concatenate([got_ref[:, c, :] for c in range(3)], axis=0)
    sums = lax.dot_general(moments, far_ref[...], nt, precision=HIGH, preferred_element_type=F32)
    line = lax.broadcasted_iota(jnp.int32, (ROWS, 4 * MODES), 0)
    carry = jnp.zeros((ROWS, 4 * MODES), F32)
    for index in range(3):
        for c in range(3):
            part = mix_ref[2 * index + (c == 2)] * sums[c * slabs:(c + 1) * slabs]
            carry = jnp.where(line == 8 * index + c, jnp.sum(part, axis=0, keepdims=True), carry)
    plain = (((1,), (0,)), ((), ()))
    incoming = lax.dot_general(carry, near_ref[...], plain, precision=HIGH, preferred_element_type=F32)
    ahead = slot_of(jnp.maximum(slab - 1, 0), slabs)
    behind = slot_of(jnp.minimum(slab + 1, slabs - 1), slabs)
    near_moments = jnp.concatenate([got_ref[ahead, 0:8, :], got_ref[slot_of(slab, slabs), 0:8, :], got_ref[behind, 0:8, :]], axis=0)
    local_kick = lax.dot_general(near_moments, local_ref[...], plain, precision=HIGH, preferred_element_type=F32)
    wide = lax.broadcasted_iota(jnp.int32, (ROWS, LANES), 0)
    kicks = jnp.where(wide % 8 == 2, local_kick[:, LANES:], local_kick[:, :LANES]) + incoming
    kick_ref[...] = kicks[8:11]
    copies = [pltpu.make_async_copy(kick_ref, kick_hbm, sems.at[0])]
    copies[0].start()

    for q in range(6):
        work_ref[q * ROWS:q * ROWS + edge, :] = got_ref[behind, edge * (q + 1):edge * (q + 2), :]
        work_ref[q * ROWS + edge:q * ROWS + edge + tiles, :] = dense_ref[q * tiles:(q + 1) * tiles, :]
        work_ref[q * ROWS + edge + tiles:q * ROWS + 2 * edge + tiles, :] = got_ref[ahead, edge * (q + 1):edge * (q + 2), :]
        work_ref[q * ROWS + 2 * edge + tiles:(q + 1) * ROWS, :] = jnp.zeros((ROWS - 2 * edge - tiles, LANES), F32)
    base = 6 * ROWS
    none = F32(-1.0)
    work_ref[base:base + edge, :] = jnp.where(slab < slabs - 1, got_ref[behind, 7 * edge:8 * edge, :], none)
    work_ref[base + edge:base + edge + tiles, :] = dense_ref[6 * tiles:7 * tiles, :]
    work_ref[base + edge + tiles:base + 2 * edge + tiles, :] = jnp.where(slab > 0, got_ref[ahead, 7 * edge:8 * edge, :], none)
    work_ref[base + 2 * edge + tiles:base + ROWS, :] = jnp.full((ROWS - 2 * edge - tiles, LANES), -1.0, F32)

    marks = work_ref[base:base + ROWS, :]
    kept = marks >= 0.0
    index = jnp.maximum(marks, 0.0).astype(jnp.int32)

    def kick_of(c):
        table = jnp.where(wide < edge, kicks[16 + c:17 + c], jnp.where(wide < edge + tiles, kicks[8 + c:9 + c], kicks[c:c + 1]))
        return jnp.take_along_axis(table, index, axis=1)

    x, px, y, py, s, e = [work_ref[q * ROWS:(q + 1) * ROWS, :] for q in range(6)]
    px = px + kick_of(0)
    py = py + kick_of(1)
    e = e + kick_of(2)
    jx = 0.5 * (x * x + px * px)
    jy = 0.5 * (y * y + py * py)
    ux = turn_reduce(0.269 + 0.05 * e + 0.02 * e * e + 0.03 * jx - 0.02 * jy)
    uy = turn_reduce(0.355 + 0.04 * e - 0.015 * e * e + 0.03 * jy - 0.02 * jx)
    cx, sx, cy, sy = cosine(ux), sine(ux), cosine(uy), sine(uy)
    e_new = e - 0.05 * (sine(radians_to_turns(0.3 + s)) - F32(math.sin(0.3)))
    s_new = s - 0.1 * e_new
    results = (cx * x + sx * px, cx * px - sx * x, cy * y + sy * py, cy * py - sy * y, s_new, e_new)
    for q, value in enumerate(results):
        done_ref[q * ROWS:(q + 1) * ROWS, :] = jnp.where(kept, value, F32(0.0))
    for tile in range(tiles + 2 * edge):
        out_ref[:, tile * LANES:(tile + 1) * LANES] = done_ref[pl.ds(tile, 6, stride=ROWS), :]
        if tile + 1 in CUTS:
            piece = slice(([0] + [cut for cut in CUTS if cut <= tile])[-1] * LANES, (tile + 1) * LANES)
            copies.append(pltpu.make_async_copy(out_ref.at[:, piece], out_hbm.at[:, piece], sems.at[len(copies)]))
            copies[-1].start()
    for copy in copies:
        copy.wait()


def specs(*kinds):
    return [pl.BlockSpec(memory_space={"s": pltpu.SMEM, "v": pltpu.VMEM, "h": pltpu.HBM}[kind]) for kind in kinds]


def stay(array):
    return pltpu.with_memory_space_constraint(array, pltpu.HBM)


def shape_of(*dims):
    return jax.ShapeDtypeStruct(dims, F32)


def outward(members):
    chips = members // 2
    ring = [FIRST_MEMBER // 2]
    for step in range(1, chips // 2 + 1):
        ring += [(ring[0] + step) % chips, (ring[0] - step) % chips]
    return [2 * chip + core for chip in dict.fromkeys(ring) for core in (1, 0)]


def body(particles, slice_index, moving, decay_rate, wake_freq, wake_amp):
    slabs = lax.axis_size("gz")
    members = lax.axis_size("pa")
    local = particles.shape[1]
    capacity = local * 3 // 16
    tiles = local // LANES
    fill = local * members / LANES
    slab = lax.axis_index("gz").astype(jnp.int32).reshape(1)
    index = slice_index.reshape(tiles, LANES)

    moments, dense, head, tail, near, far, toeplitz, mix = pl.pallas_call(
        functools.partial(deposit_kernel, slabs, local, capacity, fill),
        out_shape=[shape_of(3 * members, LANES), shape_of(7 * tiles, LANES), shape_of(ROWS, LANES), shape_of(ROWS, LANES),
                   shape_of(32, LANES), shape_of(32, LANES), shape_of(LANES, 2 * LANES), shape_of(6, slabs, 4 * MODES)],
        in_specs=specs(*"shhhhhh"),
        out_specs=specs(*"vvvvvvvv"),
        scratch_shapes=[pltpu.VMEM((6, local), F32), pltpu.VMEM((tiles, LANES), jnp.int32), pltpu.SMEM((1, 1, 2), jnp.int32),
                        pltpu.SMEM((MODES,), F32), pltpu.SMEM((MODES,), F32), pltpu.SMEM((4, MODES), F32),
                        pltpu.SemaphoreType.DMA((6,))],
        compiler_params=SMALL,
        name="deposit",
    )(slab, *[stay(array) for array in (particles, index, moving, decay_rate, wake_freq, wake_amp)])

    order = [slab_of(slot, slabs) for slot in range(slabs)]
    gathered = lax.all_to_all(moments.reshape(members, 1, 3 * LANES), "pa", 0, 0, axis_index_groups=[outward(members)])
    packed = pl.pallas_call(
        functools.partial(pack_kernel, slabs),
        out_shape=shape_of(slabs, ROWS, LANES),
        in_specs=specs(*"svvv"),
        out_specs=specs("v")[0],
        compiler_params=SMALL,
        name="pack",
    )(slab, gathered, head, tail)
    everyone = lax.all_to_all(packed, "gz", 0, 0, axis_index_groups=[order])
    return pl.pallas_call(
        functools.partial(finish_kernel, slabs, local, capacity),
        out_shape=[shape_of(3, LANES), shape_of(6, local + 2 * capacity)],
        in_specs=specs(*"svvvvvv"),
        out_specs=specs(*"hh"),
        scratch_shapes=[pltpu.VMEM((7 * ROWS, LANES), F32), pltpu.VMEM((6 * ROWS, LANES), F32), pltpu.VMEM((3, LANES), F32),
                        pltpu.VMEM((6, local + 2 * capacity), F32), pltpu.SemaphoreType.DMA((1 + len(CUTS),))],
        compiler_params=SMALL,
        name="finish",
    )(slab, everyone, dense, near, far, toeplitz, mix)


def solution(mesh):
    return jax.shard_map(
        body,
        mesh=mesh,
        in_specs=(P(None, ("gz", "pa")), P(("gz", "pa")), P("gz", "pa", None), P(), P(), P()),
        out_specs=(P(None, "gz"), P(None, ("gz", "pa"))),
        check_vma=False,
    )
```

```python
import functools
import math

import jax
import jax.numpy as jnp
from jax import lax
from jax.experimental import pallas as pl
from jax.experimental.pallas import tpu as pltpu
from jax.sharding import PartitionSpec as P

LANES = 128
MODES = 8
ROWS = 24
HIGH = lax.Precision.HIGHEST
F32 = jnp.float32

COS_TERMS = (1.0, -19.73920440673828, 64.93911743164062, -85.45014190673828, 60.167633056640625,
             -25.967601776123047, 6.528658866882324)
SIN_TERMS = (6.2831854820251465, -41.34170150756836, 81.60513305664062, -76.70301818847656,
             42.02592849731445, -14.899847984313965, 3.238137722015381)
SMALL = pltpu.CompilerParams(vmem_limit_bytes=4 << 20)
FIRST_MEMBER = 19
CUTS = (8, 22)
FIRST_SLAB = 10
INV_TWO_PI = 0.15915494309189535
TURN_PARTS = (6.28125, 1.93500518798828125e-3, 3.0199159819567529e-7)


def horner(terms, t):
    total = jnp.full_like(t, terms[-1])
    for term in terms[-2::-1]:
        total = total * t + F32(term)
    return total


def turn_reduce(turns):
    return turns - jnp.floor(turns + F32(0.5))


def sine(turns):
    return turns * horner(SIN_TERMS, turns * turns)


def cosine(turns):
    return horner(COS_TERMS, turns * turns)


def radians_to_turns(angle):
    whole = jnp.floor(angle * F32(INV_TWO_PI) + F32(0.5))
    rest = angle
    for part in TURN_PARTS:
        rest = rest - whole * F32(part)
    return rest * F32(INV_TWO_PI)


def powers(damping, freq, distance):
    envelope = jnp.exp(-damping * distance)
    turns = radians_to_turns(freq * distance)
    return envelope * cosine(turns), envelope * sine(turns)


def complex_mul(a, b):
    return a[0] * b[0] - a[1] * b[1], a[0] * b[1] + a[1] * b[0]


def spread(read, shape, axis):
    where = lax.broadcasted_iota(jnp.int32, shape, axis) % MODES
    total = jnp.zeros(shape, F32)
    for mode in range(MODES):
        total = jnp.where(where == mode, read(mode), total)
    return total


def make_tables(slabs, width, slab_ref, decay_ref, freq_ref, amp_ref, near_ref, far_ref, local_ref, mix_ref):
    shape = (MODES, LANES)
    scale = F32(1.0 / (slabs * width))
    damping = spread(lambda m: decay_ref[m], shape, 0) * scale
    freq = spread(lambda m: freq_ref[m], shape, 0)
    amps = [spread(functools.partial(lambda row, m: amp_ref[row, m], row), shape, 0) for row in range(4)]
    distance = lax.broadcasted_iota(jnp.int32, shape, 1).astype(F32)
    near = powers(damping, freq, distance)
    far = powers(damping, freq, F32(width) - distance)
    for block, half in enumerate((0, 1, 1, 0)):
        far_ref[8 * block:8 * block + 8, :] = far[half]
        near_ref[8 * block:8 * block + 8, :] = near[0] if block % 2 == 0 else -near[1]
    norm_trans = jnp.sqrt(2.0 * damping)
    norm_long = jnp.sqrt(damping * damping + freq * freq)
    wave_trans = jnp.sum(norm_trans * (amps[0] * near[0] - amps[1] * near[1]), axis=0, keepdims=True)
    wave_long = jnp.sum(norm_long * (amps[2] * near[0] - amps[3] * near[1]), axis=0, keepdims=True)
    square = (LANES, LANES)
    later = lax.broadcasted_iota(jnp.int32, square, 1) > lax.broadcasted_iota(jnp.int32, square, 0)
    for kind, wave in enumerate((wave_trans, wave_long)):
        shifted = pltpu.roll(jnp.broadcast_to(wave, square), 0, 1, stride=1, stride_axis=0)
        local_ref[:, kind * LANES:(kind + 1) * LANES] = jnp.where(later, shifted, F32(0.0))

    small = (slabs, 4 * MODES)
    damping = spread(lambda m: decay_ref[m], small, 1) * scale
    freq = spread(lambda m: freq_ref[m], small, 1)
    amps = [spread(functools.partial(lambda row, m: amp_ref[row, m], row), small, 1) for row in range(4)]
    norm_trans = jnp.sqrt(2.0 * damping)
    norm_long = jnp.sqrt(damping * damping + freq * freq)
    coefs = (amps[0] * norm_trans, amps[1] * norm_trans), (amps[2] * norm_long, amps[3] * norm_long)
    lane = lax.broadcasted_iota(jnp.int32, small, 1)
    sign = jnp.where(lane < 3 * MODES, F32(-1.0), F32(1.0))
    step = powers(damping, freq, jnp.full(small, width, F32))
    ladder = [step]
    while 2 ** len(ladder) < slabs:
        ladder.append(complex_mul(ladder[-1], ladder[-1]))
    source = slab_of(lax.broadcasted_iota(jnp.int32, small, 0), slabs)
    for index in range(3):
        hops = slab_ref[0] + (index - 2) - source
        weight = (jnp.ones(small, F32), jnp.zeros(small, F32))
        for bit, factor in enumerate(ladder):
            longer = complex_mul(weight, factor)
            taken = (hops & (1 << bit)) != 0
            weight = tuple(jnp.where(taken, b, a) for a, b in zip(weight, longer))
        for kind, coef in enumerate(coefs):
            mixed = complex_mul(weight, coef)
            both = jnp.where(lane < 2 * MODES, mixed[0], sign * mixed[1])
            mix_ref[2 * index + kind] = jnp.where(hops >= 0, both, F32(0.0))


def slab_of(slot, slabs):
    return (slot + FIRST_SLAB) % slabs


def slot_of(slab, slabs):
    return (slab + slabs - FIRST_SLAB) % slabs


def fetch(sources, targets, sems):
    copies = [pltpu.make_async_copy(a, b, sems.at[k]) for k, (a, b) in enumerate(zip(sources, targets))]
    for copy in copies:
        copy.start()
    for copy in copies:
        copy.wait()


def deposit(local, fill, part_ref, index_ref, moment_ref):
    tiles = local // LANES
    shape = (8, local)
    row = lax.broadcasted_iota(jnp.int32, shape, 0)
    base = jnp.where(row < 3, part_ref[0:1, :], jnp.where(row < 6, part_ref[2:3, :], F32(1.0)))
    bf = jnp.bfloat16
    high = base.astype(bf).astype(F32)
    rest = base - high
    mid = rest.astype(bf).astype(F32)
    low = rest - mid
    third = row % 3
    values = jnp.where(third == 0, high, jnp.where(third == 1, mid, low)).astype(bf)
    slot = lax.broadcasted_iota(jnp.int32, (LANES, LANES), 0)
    total = jnp.zeros((8, LANES), F32)
    group = 8
    for first in range(0, tiles, group):
        hot = jnp.concatenate(
            [(slot == index_ref[t:t + 1, :]).astype(F32).astype(bf) for t in range(first, first + group)], axis=1
        )
        total = total + lax.dot_general(
            values[:, first * LANES:(first + group) * LANES], hot, (((1,), (1,)), ((), ())), preferred_element_type=F32
        )
    root = F32(1.0 / math.sqrt(fill))
    sums = (
        (total[0:1] + total[1:2] + total[2:3]) * root,
        (total[3:4] + total[4:5] + total[5:6]) * root,
        total[6:7] * F32(1.0 / fill),
    )
    third = lax.broadcasted_iota(jnp.int32, (ROWS, LANES), 0) % 3
    block = jnp.where(third == 0, sums[0], jnp.where(third == 1, sums[1], sums[2]))
    for start in range(0, moment_ref.shape[0], ROWS):
        moment_ref[start:start + ROWS, :] = block


def make_payload(local, capacity, part_ref, index_ref, moving_ref, dense_ref, head_ref, tail_ref):
    tiles = local // LANES
    for tile in range(tiles):
        dense_ref[pl.ds(tile, 6, stride=tiles), :] = part_ref[:, tile * LANES:(tile + 1) * LANES]
    own = (tiles, LANES)
    position = lax.broadcasted_iota(jnp.int32, own, 0) * LANES + lax.broadcasted_iota(jnp.int32, own, 1)
    stays = (position >= moving_ref[0, 0, 0]) & (position < local - moving_ref[0, 0, 1])
    dense_ref[6 * tiles:7 * tiles, :] = jnp.where(stays, index_ref[...].astype(F32), F32(-1.0))
    edge = capacity // LANES
    place = lax.broadcasted_iota(jnp.int32, (edge, LANES), 0) * LANES + lax.broadcasted_iota(jnp.int32, (edge, LANES), 1)
    for ref, start, leaving in (
        (head_ref, 0, place < moving_ref[0, 0, 0]),
        (tail_ref, tiles - edge, place >= capacity - moving_ref[0, 0, 1]),
    ):
        ref[0:edge, :] = jnp.zeros((edge, LANES), F32)
        for q in range(6):
            ref[edge * (q + 1):edge * (q + 2), :] = dense_ref[q * tiles + start:q * tiles + start + edge, :]
        ref[edge * 7:edge * 8, :] = jnp.where(leaving, index_ref[start:start + edge, :].astype(F32), F32(-1.0))


def deposit_kernel(slabs, local, capacity, fill, slab_ref, part_hbm, index_hbm, moving_hbm, decay_hbm, freq_hbm, amp_hbm, *refs):
    outs, (part_ref, index_ref, moving_ref, decay_ref, freq_ref, amp_ref, sems) = refs[:8], refs[8:]
    fetch((part_hbm, index_hbm, moving_hbm, decay_hbm, freq_hbm, amp_hbm),
          (part_ref, index_ref, moving_ref, decay_ref, freq_ref, amp_ref), sems)
    deposit(local, fill, part_ref, index_ref, outs[0])
    make_payload(local, capacity, part_ref, index_ref, moving_ref, *outs[1:4])
    make_tables(slabs, LANES, slab_ref, decay_ref, freq_ref, amp_ref, *outs[4:])


def pack_kernel(slabs, slab_ref, got_ref, head_ref, tail_ref, out_ref):
    moments = got_ref[0]
    for source in range(1, got_ref.shape[0]):
        moments = moments + got_ref[source]
    head, tail = head_ref[...], tail_ref[...]
    for slot in range(slabs):
        out_ref[slot] = jnp.where(slab_of(slot, slabs) < slab_ref[0], head, tail)
        for c in range(3):
            out_ref[slot, c:c + 1, :] = moments[:, c * LANES:(c + 1) * LANES]


def finish_kernel(slabs, local, capacity, slab_ref, got_ref, dense_ref, near_ref, far_ref, local_ref, mix_ref, kick_hbm, out_hbm, work_ref, done_ref, kick_ref, out_ref, sems):
    tiles = local // LANES
    edge = capacity // LANES
    slab = slab_ref[0]
    nt = (((1,), (1,)), ((), ()))
    moments = jnp.concatenate([got_ref[:, c, :] for c in range(3)], axis=0)
    sums = lax.dot_general(moments, far_ref[...], nt, precision=HIGH, preferred_element_type=F32)
    line = lax.broadcasted_iota(jnp.int32, (ROWS, 4 * MODES), 0)
    carry = jnp.zeros((ROWS, 4 * MODES), F32)
    for index in range(3):
        for c in range(3):
            part = mix_ref[2 * index + (c == 2)] * sums[c * slabs:(c + 1) * slabs]
            carry = jnp.where(line == 8 * index + c, jnp.sum(part, axis=0, keepdims=True), carry)
    plain = (((1,), (0,)), ((), ()))
    incoming = lax.dot_general(carry, near_ref[...], plain, precision=HIGH, preferred_element_type=F32)
    ahead = slot_of(jnp.maximum(slab - 1, 0), slabs)
    behind = slot_of(jnp.minimum(slab + 1, slabs - 1), slabs)
    near_moments = jnp.concatenate([got_ref[ahead, 0:8, :], got_ref[slot_of(slab, slabs), 0:8, :], got_ref[behind, 0:8, :]], axis=0)
    local_kick = lax.dot_general(near_moments, local_ref[...], plain, precision=HIGH, preferred_element_type=F32)
    wide = lax.broadcasted_iota(jnp.int32, (ROWS, LANES), 0)
    kicks = jnp.where(wide % 8 == 2, local_kick[:, LANES:], local_kick[:, :LANES]) + incoming
    kick_ref[...] = kicks[8:11]
    copies = [pltpu.make_async_copy(kick_ref, kick_hbm, sems.at[0])]
    copies[0].start()

    for q in range(6):
        work_ref[q * ROWS:q * ROWS + edge, :] = got_ref[behind, edge * (q + 1):edge * (q + 2), :]
        work_ref[q * ROWS + edge:q * ROWS + edge + tiles, :] = dense_ref[q * tiles:(q + 1) * tiles, :]
        work_ref[q * ROWS + edge + tiles:q * ROWS + 2 * edge + tiles, :] = got_ref[ahead, edge * (q + 1):edge * (q + 2), :]
        work_ref[q * ROWS + 2 * edge + tiles:(q + 1) * ROWS, :] = jnp.zeros((ROWS - 2 * edge - tiles, LANES), F32)
    base = 6 * ROWS
    none = F32(-1.0)
    work_ref[base:base + edge, :] = jnp.where(slab < slabs - 1, got_ref[behind, 7 * edge:8 * edge, :], none)
    work_ref[base + edge:base + edge + tiles, :] = dense_ref[6 * tiles:7 * tiles, :]
    work_ref[base + edge + tiles:base + 2 * edge + tiles, :] = jnp.where(slab > 0, got_ref[ahead, 7 * edge:8 * edge, :], none)
    work_ref[base + 2 * edge + tiles:base + ROWS, :] = jnp.full((ROWS - 2 * edge - tiles, LANES), -1.0, F32)

    marks = work_ref[base:base + ROWS, :]
    kept = marks >= 0.0
    index = jnp.maximum(marks, 0.0).astype(jnp.int32)

    def kick_of(c):
        table = jnp.where(wide < edge, kicks[16 + c:17 + c], jnp.where(wide < edge + tiles, kicks[8 + c:9 + c], kicks[c:c + 1]))
        return jnp.take_along_axis(table, index, axis=1)

    x, px, y, py, s, e = [work_ref[q * ROWS:(q + 1) * ROWS, :] for q in range(6)]
    px = px + kick_of(0)
    py = py + kick_of(1)
    e = e + kick_of(2)
    jx = 0.5 * (x * x + px * px)
    jy = 0.5 * (y * y + py * py)
    ux = turn_reduce(0.269 + 0.05 * e + 0.02 * e * e + 0.03 * jx - 0.02 * jy)
    uy = turn_reduce(0.355 + 0.04 * e - 0.015 * e * e + 0.03 * jy - 0.02 * jx)
    cx, sx, cy, sy = cosine(ux), sine(ux), cosine(uy), sine(uy)
    e_new = e - 0.05 * (sine(radians_to_turns(0.3 + s)) - F32(math.sin(0.3)))
    s_new = s - 0.1 * e_new
    results = (cx * x + sx * px, cx * px - sx * x, cy * y + sy * py, cy * py - sy * y, s_new, e_new)
    for q, value in enumerate(results):
        done_ref[q * ROWS:(q + 1) * ROWS, :] = jnp.where(kept, value, F32(0.0))
    for tile in range(tiles + 2 * edge):
        out_ref[:, tile * LANES:(tile + 1) * LANES] = done_ref[pl.ds(tile, 6, stride=ROWS), :]
        if tile + 1 in CUTS:
            piece = slice(([0] + [cut for cut in CUTS if cut <= tile])[-1] * LANES, (tile + 1) * LANES)
            copies.append(pltpu.make_async_copy(out_ref.at[:, piece], out_hbm.at[:, piece], sems.at[len(copies)]))
            copies[-1].start()
    for copy in copies:
        copy.wait()


def specs(*kinds):
    return [pl.BlockSpec(memory_space={"s": pltpu.SMEM, "v": pltpu.VMEM, "h": pltpu.HBM}[kind]) for kind in kinds]


def stay(array):
    return pltpu.with_memory_space_constraint(array, pltpu.HBM)


def shape_of(*dims):
    return jax.ShapeDtypeStruct(dims, F32)


def outward(members):
    chips = members // 2
    ring = [FIRST_MEMBER // 2]
    for step in range(1, chips // 2 + 1):
        ring += [(ring[0] + step) % chips, (ring[0] - step) % chips]
    return [2 * chip + core for chip in dict.fromkeys(ring) for core in (1, 0)]


def body(particles, slice_index, moving, decay_rate, wake_freq, wake_amp):
    slabs = lax.axis_size("gz")
    members = lax.axis_size("pa")
    local = particles.shape[1]
    capacity = local * 3 // 16
    tiles = local // LANES
    fill = local * members / LANES
    slab = lax.axis_index("gz").astype(jnp.int32).reshape(1)
    index = slice_index.reshape(tiles, LANES)

    moments, dense, head, tail, near, far, toeplitz, mix = pl.pallas_call(
        functools.partial(deposit_kernel, slabs, local, capacity, fill),
        out_shape=[shape_of(3 * members, LANES), shape_of(7 * tiles, LANES), shape_of(ROWS, LANES), shape_of(ROWS, LANES),
                   shape_of(32, LANES), shape_of(32, LANES), shape_of(LANES, 2 * LANES), shape_of(6, slabs, 4 * MODES)],
        in_specs=specs(*"shhhhhh"),
        out_specs=specs(*"vvvvvvvv"),
        scratch_shapes=[pltpu.VMEM((6, local), F32), pltpu.VMEM((tiles, LANES), jnp.int32), pltpu.SMEM((1, 1, 2), jnp.int32),
                        pltpu.SMEM((MODES,), F32), pltpu.SMEM((MODES,), F32), pltpu.SMEM((4, MODES), F32),
                        pltpu.SemaphoreType.DMA((6,))],
        compiler_params=SMALL,
        name="deposit",
    )(slab, *[stay(array) for array in (particles, index, moving, decay_rate, wake_freq, wake_amp)])

    order = [slab_of(slot, slabs) for slot in range(slabs)]
    gathered = lax.all_to_all(moments.reshape(members, 1, 3 * LANES), "pa", 0, 0, axis_index_groups=[outward(members)])
    packed = pl.pallas_call(
        functools.partial(pack_kernel, slabs),
        out_shape=shape_of(slabs, ROWS, LANES),
        in_specs=specs(*"svvv"),
        out_specs=specs("v")[0],
        compiler_params=SMALL,
        name="pack",
    )(slab, gathered, head, tail)
    everyone = lax.all_to_all(packed, "gz", 0, 0, axis_index_groups=[order])
    return pl.pallas_call(
        functools.partial(finish_kernel, slabs, local, capacity),
        out_shape=[shape_of(3, LANES), shape_of(6, local + 2 * capacity)],
        in_specs=specs(*"svvvvvv"),
        out_specs=specs(*"hh"),
        scratch_shapes=[pltpu.VMEM((7 * ROWS, LANES), F32), pltpu.VMEM((6 * ROWS, LANES), F32), pltpu.VMEM((3, LANES), F32),
                        pltpu.VMEM((6, local + 2 * capacity), F32), pltpu.SemaphoreType.DMA((1 + len(CUTS),))],
        compiler_params=SMALL,
        name="finish",
    )(slab, everyone, dense, near, far, toeplitz, mix)


def solution(mesh):
    return jax.shard_map(
        body,
        mesh=mesh,
        in_specs=(P(None, ("gz", "pa")), P(("gz", "pa")), P("gz", "pa", None), P(), P(), P()),
        out_specs=(P(None, "gz"), P(None, ("gz", "pa"))),
        check_vma=False,
    )
```

```python
import functools
import math

import jax
import jax.numpy as jnp
from jax import lax
from jax.experimental import pallas as pl
from jax.experimental.pallas import tpu as pltpu
from jax.sharding import PartitionSpec as P

LANES = 128
MODES = 8
ROWS = 24
HIGH = lax.Precision.HIGHEST
F32 = jnp.float32

COS_TERMS = (1.0, -19.73920440673828, 64.93911743164062, -85.45014190673828, 60.167633056640625,
             -25.967601776123047, 6.528658866882324)
SIN_TERMS = (6.2831854820251465, -41.34170150756836, 81.60513305664062, -76.70301818847656,
             42.02592849731445, -14.899847984313965, 3.238137722015381)
SMALL = pltpu.CompilerParams(vmem_limit_bytes=4 << 20)
FIRST_MEMBER = 19
CUTS = (8, 22)
FIRST_SLAB = 10
INV_TWO_PI = 0.15915494309189535
TURN_PARTS = (6.28125, 1.93500518798828125e-3, 3.0199159819567529e-7)


def horner(terms, t):
    total = jnp.full_like(t, terms[-1])
    for term in terms[-2::-1]:
        total = total * t + F32(term)
    return total


def turn_reduce(turns):
    return turns - jnp.floor(turns + F32(0.5))


def sine(turns):
    return turns * horner(SIN_TERMS, turns * turns)


def cosine(turns):
    return horner(COS_TERMS, turns * turns)


def radians_to_turns(angle):
    whole = jnp.floor(angle * F32(INV_TWO_PI) + F32(0.5))
    rest = angle
    for part in TURN_PARTS:
        rest = rest - whole * F32(part)
    return rest * F32(INV_TWO_PI)


def powers(damping, freq, distance):
    envelope = jnp.exp(-damping * distance)
    turns = radians_to_turns(freq * distance)
    return envelope * cosine(turns), envelope * sine(turns)


def complex_mul(a, b):
    return a[0] * b[0] - a[1] * b[1], a[0] * b[1] + a[1] * b[0]


def spread(read, shape, axis):
    where = lax.broadcasted_iota(jnp.int32, shape, axis) % MODES
    total = jnp.zeros(shape, F32)
    for mode in range(MODES):
        total = jnp.where(where == mode, read(mode), total)
    return total


def make_tables(slabs, width, slab_ref, decay_ref, freq_ref, amp_ref, near_ref, far_ref, local_ref, mix_ref):
    shape = (MODES, LANES)
    scale = F32(1.0 / (slabs * width))
    damping = spread(lambda m: decay_ref[m], shape, 0) * scale
    freq = spread(lambda m: freq_ref[m], shape, 0)
    amps = [spread(functools.partial(lambda row, m: amp_ref[row, m], row), shape, 0) for row in range(4)]
    distance = lax.broadcasted_iota(jnp.int32, shape, 1).astype(F32)
    near = powers(damping, freq, distance)
    far = powers(damping, freq, F32(width) - distance)
    for block, half in enumerate((0, 1, 1, 0)):
        far_ref[8 * block:8 * block + 8, :] = far[half]
        near_ref[8 * block:8 * block + 8, :] = near[0] if block % 2 == 0 else -near[1]
    norm_trans = jnp.sqrt(2.0 * damping)
    norm_long = jnp.sqrt(damping * damping + freq * freq)
    wave_trans = jnp.sum(norm_trans * (amps[0] * near[0] - amps[1] * near[1]), axis=0, keepdims=True)
    wave_long = jnp.sum(norm_long * (amps[2] * near[0] - amps[3] * near[1]), axis=0, keepdims=True)
    square = (LANES, LANES)
    later = lax.broadcasted_iota(jnp.int32, square, 1) > lax.broadcasted_iota(jnp.int32, square, 0)
    for kind, wave in enumerate((wave_trans, wave_long)):
        shifted = pltpu.roll(jnp.broadcast_to(wave, square), 0, 1, stride=1, stride_axis=0)
        local_ref[:, kind * LANES:(kind + 1) * LANES] = jnp.where(later, shifted, F32(0.0))

    small = (slabs, 4 * MODES)
    damping = spread(lambda m: decay_ref[m], small, 1) * scale
    freq = spread(lambda m: freq_ref[m], small, 1)
    amps = [spread(functools.partial(lambda row, m: amp_ref[row, m], row), small, 1) for row in range(4)]
    norm_trans = jnp.sqrt(2.0 * damping)
    norm_long = jnp.sqrt(damping * damping + freq * freq)
    coefs = (amps[0] * norm_trans, amps[1] * norm_trans), (amps[2] * norm_long, amps[3] * norm_long)
    lane = lax.broadcasted_iota(jnp.int32, small, 1)
    sign = jnp.where(lane < 3 * MODES, F32(-1.0), F32(1.0))
    step = powers(damping, freq, jnp.full(small, width, F32))
    ladder = [step]
    while 2 ** len(ladder) < slabs:
        ladder.append(complex_mul(ladder[-1], ladder[-1]))
    source = slab_of(lax.broadcasted_iota(jnp.int32, small, 0), slabs)
    for index in range(3):
        hops = slab_ref[0] + (index - 2) - source
        weight = (jnp.ones(small, F32), jnp.zeros(small, F32))
        for bit, factor in enumerate(ladder):
            longer = complex_mul(weight, factor)
            taken = (hops & (1 << bit)) != 0
            weight = tuple(jnp.where(taken, b, a) for a, b in zip(weight, longer))
        for kind, coef in enumerate(coefs):
            mixed = complex_mul(weight, coef)
            both = jnp.where(lane < 2 * MODES, mixed[0], sign * mixed[1])
            mix_ref[2 * index + kind] = jnp.where(hops >= 0, both, F32(0.0))


def slab_of(slot, slabs):
    return (slot + FIRST_SLAB) % slabs


def slot_of(slab, slabs):
    return (slab + slabs - FIRST_SLAB) % slabs


def fetch(sources, targets, sems):
    copies = [pltpu.make_async_copy(a, b, sems.at[k]) for k, (a, b) in enumerate(zip(sources, targets))]
    for copy in copies:
        copy.start()
    for copy in copies:
        copy.wait()


def deposit(local, fill, part_ref, index_ref, moment_ref):
    tiles = local // LANES
    shape = (8, local)
    row = lax.broadcasted_iota(jnp.int32, shape, 0)
    base = jnp.where(row < 3, part_ref[0:1, :], jnp.where(row < 6, part_ref[2:3, :], F32(1.0)))
    bf = jnp.bfloat16
    high = base.astype(bf).astype(F32)
    rest = base - high
    mid = rest.astype(bf).astype(F32)
    low = rest - mid
    third = row % 3
    values = jnp.where(third == 0, high, jnp.where(third == 1, mid, low)).astype(bf)
    slot = lax.broadcasted_iota(jnp.int32, (LANES, LANES), 0)
    total = jnp.zeros((8, LANES), F32)
    group = 8
    for first in range(0, tiles, group):
        hot = jnp.concatenate(
            [(slot == index_ref[t:t + 1, :]).astype(F32).astype(bf) for t in range(first, first + group)], axis=1
        )
        total = total + lax.dot_general(
            values[:, first * LANES:(first + group) * LANES], hot, (((1,), (1,)), ((), ())), preferred_element_type=F32
        )
    root = F32(1.0 / math.sqrt(fill))
    sums = (
        (total[0:1] + total[1:2] + total[2:3]) * root,
        (total[3:4] + total[4:5] + total[5:6]) * root,
        total[6:7] * F32(1.0 / fill),
    )
    third = lax.broadcasted_iota(jnp.int32, (ROWS, LANES), 0) % 3
    block = jnp.where(third == 0, sums[0], jnp.where(third == 1, sums[1], sums[2]))
    for start in range(0, moment_ref.shape[0], ROWS):
        moment_ref[start:start + ROWS, :] = block


def make_payload(local, capacity, part_ref, index_ref, moving_ref, dense_ref, head_ref, tail_ref):
    tiles = local // LANES
    for tile in range(tiles):
        dense_ref[pl.ds(tile, 6, stride=tiles), :] = part_ref[:, tile * LANES:(tile + 1) * LANES]
    own = (tiles, LANES)
    position = lax.broadcasted_iota(jnp.int32, own, 0) * LANES + lax.broadcasted_iota(jnp.int32, own, 1)
    stays = (position >= moving_ref[0, 0, 0]) & (position < local - moving_ref[0, 0, 1])
    dense_ref[6 * tiles:7 * tiles, :] = jnp.where(stays, index_ref[...].astype(F32), F32(-1.0))
    edge = capacity // LANES
    place = lax.broadcasted_iota(jnp.int32, (edge, LANES), 0) * LANES + lax.broadcasted_iota(jnp.int32, (edge, LANES), 1)
    for ref, start, leaving in (
        (head_ref, 0, place < moving_ref[0, 0, 0]),
        (tail_ref, tiles - edge, place >= capacity - moving_ref[0, 0, 1]),
    ):
        ref[0:edge, :] = jnp.zeros((edge, LANES), F32)
        for q in range(6):
            ref[edge * (q + 1):edge * (q + 2), :] = dense_ref[q * tiles + start:q * tiles + start + edge, :]
        ref[edge * 7:edge * 8, :] = jnp.where(leaving, index_ref[start:start + edge, :].astype(F32), F32(-1.0))


def deposit_kernel(slabs, local, capacity, fill, slab_ref, part_hbm, index_hbm, moving_hbm, decay_hbm, freq_hbm, amp_hbm, *refs):
    outs, (part_ref, index_ref, moving_ref, decay_ref, freq_ref, amp_ref, sems) = refs[:8], refs[8:]
    fetch((part_hbm, index_hbm, moving_hbm, decay_hbm, freq_hbm, amp_hbm),
          (part_ref, index_ref, moving_ref, decay_ref, freq_ref, amp_ref), sems)
    deposit(local, fill, part_ref, index_ref, outs[0])
    make_payload(local, capacity, part_ref, index_ref, moving_ref, *outs[1:4])
    make_tables(slabs, LANES, slab_ref, decay_ref, freq_ref, amp_ref, *outs[4:])


def pack_kernel(slabs, slab_ref, got_ref, head_ref, tail_ref, out_ref):
    moments = got_ref[0]
    for source in range(1, got_ref.shape[0]):
        moments = moments + got_ref[source]
    head, tail = head_ref[...], tail_ref[...]
    for slot in range(slabs):
        out_ref[slot] = jnp.where(slab_of(slot, slabs) < slab_ref[0], head, tail)
        for c in range(3):
            out_ref[slot, c:c + 1, :] = moments[:, c * LANES:(c + 1) * LANES]


def finish_kernel(slabs, local, capacity, slab_ref, got_ref, dense_ref, near_ref, far_ref, local_ref, mix_ref, kick_hbm, out_hbm, work_ref, done_ref, kick_ref, out_ref, sems):
    tiles = local // LANES
    edge = capacity // LANES
    slab = slab_ref[0]
    nt = (((1,), (1,)), ((), ()))
    moments = jnp.concatenate([got_ref[:, c, :] for c in range(3)], axis=0)
    sums = lax.dot_general(moments, far_ref[...], nt, precision=HIGH, preferred_element_type=F32)
    line = lax.broadcasted_iota(jnp.int32, (ROWS, 4 * MODES), 0)
    carry = jnp.zeros((ROWS, 4 * MODES), F32)
    for index in range(3):
        for c in range(3):
            part = mix_ref[2 * index + (c == 2)] * sums[c * slabs:(c + 1) * slabs]
            carry = jnp.where(line == 8 * index + c, jnp.sum(part, axis=0, keepdims=True), carry)
    plain = (((1,), (0,)), ((), ()))
    incoming = lax.dot_general(carry, near_ref[...], plain, precision=HIGH, preferred_element_type=F32)
    ahead = slot_of(jnp.maximum(slab - 1, 0), slabs)
    behind = slot_of(jnp.minimum(slab + 1, slabs - 1), slabs)
    near_moments = jnp.concatenate([got_ref[ahead, 0:8, :], got_ref[slot_of(slab, slabs), 0:8, :], got_ref[behind, 0:8, :]], axis=0)
    local_kick = lax.dot_general(near_moments, local_ref[...], plain, precision=HIGH, preferred_element_type=F32)
    wide = lax.broadcasted_iota(jnp.int32, (ROWS, LANES), 0)
    kicks = jnp.where(wide % 8 == 2, local_kick[:, LANES:], local_kick[:, :LANES]) + incoming
    kick_ref[...] = kicks[8:11]
    copies = [pltpu.make_async_copy(kick_ref, kick_hbm, sems.at[0])]
    copies[0].start()

    for q in range(6):
        work_ref[q * ROWS:q * ROWS + edge, :] = got_ref[behind, edge * (q + 1):edge * (q + 2), :]
        work_ref[q * ROWS + edge:q * ROWS + edge + tiles, :] = dense_ref[q * tiles:(q + 1) * tiles, :]
        work_ref[q * ROWS + edge + tiles:q * ROWS + 2 * edge + tiles, :] = got_ref[ahead, edge * (q + 1):edge * (q + 2), :]
        work_ref[q * ROWS + 2 * edge + tiles:(q + 1) * ROWS, :] = jnp.zeros((ROWS - 2 * edge - tiles, LANES), F32)
    base = 6 * ROWS
    none = F32(-1.0)
    work_ref[base:base + edge, :] = jnp.where(slab < slabs - 1, got_ref[behind, 7 * edge:8 * edge, :], none)
    work_ref[base + edge:base + edge + tiles, :] = dense_ref[6 * tiles:7 * tiles, :]
    work_ref[base + edge + tiles:base + 2 * edge + tiles, :] = jnp.where(slab > 0, got_ref[ahead, 7 * edge:8 * edge, :], none)
    work_ref[base + 2 * edge + tiles:base + ROWS, :] = jnp.full((ROWS - 2 * edge - tiles, LANES), -1.0, F32)

    marks = work_ref[base:base + ROWS, :]
    kept = marks >= 0.0
    index = jnp.maximum(marks, 0.0).astype(jnp.int32)

    def kick_of(c):
        table = jnp.where(wide < edge, kicks[16 + c:17 + c], jnp.where(wide < edge + tiles, kicks[8 + c:9 + c], kicks[c:c + 1]))
        return jnp.take_along_axis(table, index, axis=1)

    x, px, y, py, s, e = [work_ref[q * ROWS:(q + 1) * ROWS, :] for q in range(6)]
    px = px + kick_of(0)
    py = py + kick_of(1)
    e = e + kick_of(2)
    jx = 0.5 * (x * x + px * px)
    jy = 0.5 * (y * y + py * py)
    ux = turn_reduce(0.269 + 0.05 * e + 0.02 * e * e + 0.03 * jx - 0.02 * jy)
    uy = turn_reduce(0.355 + 0.04 * e - 0.015 * e * e + 0.03 * jy - 0.02 * jx)
    cx, sx, cy, sy = cosine(ux), sine(ux), cosine(uy), sine(uy)
    e_new = e - 0.05 * (sine(radians_to_turns(0.3 + s)) - F32(math.sin(0.3)))
    s_new = s - 0.1 * e_new
    results = (cx * x + sx * px, cx * px - sx * x, cy * y + sy * py, cy * py - sy * y, s_new, e_new)
    for q, value in enumerate(results):
        done_ref[q * ROWS:(q + 1) * ROWS, :] = jnp.where(kept, value, F32(0.0))
    for tile in range(tiles + 2 * edge):
        out_ref[:, tile * LANES:(tile + 1) * LANES] = done_ref[pl.ds(tile, 6, stride=ROWS), :]
        if tile + 1 in CUTS:
            piece = slice(([0] + [cut for cut in CUTS if cut <= tile])[-1] * LANES, (tile + 1) * LANES)
            copies.append(pltpu.make_async_copy(out_ref.at[:, piece], out_hbm.at[:, piece], sems.at[len(copies)]))
            copies[-1].start()
    for copy in copies:
        copy.wait()


def specs(*kinds):
    return [pl.BlockSpec(memory_space={"s": pltpu.SMEM, "v": pltpu.VMEM, "h": pltpu.HBM}[kind]) for kind in kinds]


def stay(array):
    return pltpu.with_memory_space_constraint(array, pltpu.HBM)


def shape_of(*dims):
    return jax.ShapeDtypeStruct(dims, F32)


def outward(members):
    chips = members // 2
    ring = [FIRST_MEMBER // 2]
    for step in range(1, chips // 2 + 1):
        ring += [(ring[0] + step) % chips, (ring[0] - step) % chips]
    rest = [2 * chip + core for chip in dict.fromkeys(ring) for core in (0, 1)]
    return [FIRST_MEMBER] + [member for member in rest if member != FIRST_MEMBER]


def body(particles, slice_index, moving, decay_rate, wake_freq, wake_amp):
    slabs = lax.axis_size("gz")
    members = lax.axis_size("pa")
    local = particles.shape[1]
    capacity = local * 3 // 16
    tiles = local // LANES
    fill = local * members / LANES
    slab = lax.axis_index("gz").astype(jnp.int32).reshape(1)
    index = slice_index.reshape(tiles, LANES)

    moments, dense, head, tail, near, far, toeplitz, mix = pl.pallas_call(
        functools.partial(deposit_kernel, slabs, local, capacity, fill),
        out_shape=[shape_of(3 * members, LANES), shape_of(7 * tiles, LANES), shape_of(ROWS, LANES), shape_of(ROWS, LANES),
                   shape_of(32, LANES), shape_of(32, LANES), shape_of(LANES, 2 * LANES), shape_of(6, slabs, 4 * MODES)],
        in_specs=specs(*"shhhhhh"),
        out_specs=specs(*"vvvvvvvv"),
        scratch_shapes=[pltpu.VMEM((6, local), F32), pltpu.VMEM((tiles, LANES), jnp.int32), pltpu.SMEM((1, 1, 2), jnp.int32),
                        pltpu.SMEM((MODES,), F32), pltpu.SMEM((MODES,), F32), pltpu.SMEM((4, MODES), F32),
                        pltpu.SemaphoreType.DMA((6,))],
        compiler_params=SMALL,
        name="deposit",
    )(slab, *[stay(array) for array in (particles, index, moving, decay_rate, wake_freq, wake_amp)])

    order = [slab_of(slot, slabs) for slot in range(slabs)]
    gathered = lax.all_to_all(moments.reshape(members, 1, 3 * LANES), "pa", 0, 0, axis_index_groups=[outward(members)])
    packed = pl.pallas_call(
        functools.partial(pack_kernel, slabs),
        out_shape=shape_of(slabs, ROWS, LANES),
        in_specs=specs(*"svvv"),
        out_specs=specs("v")[0],
        compiler_params=SMALL,
        name="pack",
    )(slab, gathered, head, tail)
    everyone = lax.all_to_all(packed, "gz", 0, 0, axis_index_groups=[order])
    return pl.pallas_call(
        functools.partial(finish_kernel, slabs, local, capacity),
        out_shape=[shape_of(3, LANES), shape_of(6, local + 2 * capacity)],
        in_specs=specs(*"svvvvvv"),
        out_specs=specs(*"hh"),
        scratch_shapes=[pltpu.VMEM((7 * ROWS, LANES), F32), pltpu.VMEM((6 * ROWS, LANES), F32), pltpu.VMEM((3, LANES), F32),
                        pltpu.VMEM((6, local + 2 * capacity), F32), pltpu.SemaphoreType.DMA((1 + len(CUTS),))],
        compiler_params=SMALL,
        name="finish",
    )(slab, everyone, dense, near, far, toeplitz, mix)


def solution(mesh):
    return jax.shard_map(
        body,
        mesh=mesh,
        in_specs=(P(None, ("gz", "pa")), P(("gz", "pa")), P("gz", "pa", None), P(), P(), P()),
        out_specs=(P(None, "gz"), P(None, ("gz", "pa"))),
        check_vma=False,
    )
```
